32 devices in a mesh: group: 2 (over y), quad: 2 (over core), rows: 8 (over z, x).
Axes of the slice: x: 2, y: 2, z: 4, core: 2. Of those that a mesh axis runs over, the one named last changes fastest.
Arguments:
- solutions: bfloat16 [32, 20480, 128], P('quad', ('group', 'rows')), parts along dimension 1, may hold values from -24 to 24
- point_of_slot: int32 [64], P(('group', 'quad')), parts along dimension 0, may hold values from 0 to 31, each once
- mass_blocks: bfloat16 [160, 20, 128, 128], P(('group', 'rows')), parts along dimension 0, may hold values from -0.125 to 0.125
- block_cols: int32 [160, 20], P(('group', 'rows')), parts along dimension 0, may hold values from 0 to 79, as said below
- sources: bfloat16 [20480, 64], P(('group', 'rows')), parts along dimension 0, may hold values from -0.0625 to 0.0625
Outputs:
- mass_applied: bfloat16 [8, 20480, 128], P('quad', ('group', 'rows')), parts along dimension 1
- reduced: float32 [16, 64, 128], P(('group', 'quad')), parts along dimension 0
The draws below stay inside these ranges and needn't reach their ends.
There are 2 independent parts, one for each index of `group`. The reference program is written for one: setup_inputs(seed, part) draws one part's arguments, and reference() takes and returns one part's arrays. A program takes and returns all parts, laid end to end along the dimension named above; each array names one. Nothing has to cross between parts.
Inputs may be any that keep to these rules, and one draw needn't show every extreme that they name: `point_of_slot`: each contour point sits in exactly one slot. `block_cols`: slot 0 of block row i holds i; every entry c of block row i has |c - i| <= 10; entries of a block row may repeat.
All inputs are finite; a program needn't handle non-finite values.
Results may differ from the reference program's by a relative error of at most 0.0063.
Values may be sent and summed in bfloat16 or wider, within the bound.
A program may use at most 128 MiB of HBM per device.

```python
import math
import jax
import jax.numpy as jnp
from jax import lax

ROWS_DEV = 1280
POINTS_DEV = 16
MOMENTS = 8
COLUMNS = 64
BLOCK = 128
SLOTS = 20
POINTS = 32
NBLOCKS = 80
ORDER = 10240
N_QUAD = 2


def draw_block_cols(key, part):
    span_blocks = ROWS_DEV // BLOCK
    row_index = jnp.arange(NBLOCKS, dtype=jnp.int32)[:, None]
    lowest = jnp.maximum(row_index - span_blocks, 0)
    highest = jnp.minimum(row_index + span_blocks, NBLOCKS - 1)
    random_bits = jax.random.randint(jax.random.fold_in(key, 7), (NBLOCKS, SLOTS - 1), 0, 1 << 20, dtype=jnp.int32)
    picked = lowest + random_bits % (highest - lowest + 1)
    return jnp.concatenate([row_index, picked], axis=1).astype(jnp.int32)


def levels(own_key, shape, cuts, smallest, high):
    def one(position, blocks):
        heights = jax.random.uniform(jax.random.fold_in(jax.random.fold_in(own_key, 6), position), (blocks,), jnp.float32, smallest / len(cuts), high / len(cuts))
        return jnp.repeat(jnp.exp(heights), shape[position] // blocks).reshape((-1,) + (1,) * (len(shape) - position - 1))

    factor_of = one(*cuts[0])
    for cut in cuts[1:]:
        factor_of = factor_of * one(*cut)
    return factor_of


def gaussian(stream_key, extent, spread, reach, pieces=(), kind=jnp.bfloat16):
    array = spread * jax.random.normal(stream_key, extent, jnp.float32)
    if pieces:
        array = array * levels(stream_key, extent, pieces, -0.22, 0.18)
    return jnp.clip(array, -reach, reach).astype(kind)


def setup_inputs(seed: int = 0, part: int = 0) -> dict:
    splits = jax.random.split(jax.random.key(seed), 6)
    part_splits = jax.random.split(jax.random.fold_in(splits[5], part), 6)
    return {
        "solutions": gaussian(part_splits[0], (POINTS, ORDER, 2 * COLUMNS), 4.0, 24.0, ((0, 2), (1, 8))),
        "point_of_slot": jax.random.permutation(part_splits[1], POINTS).astype(jnp.int32),
        "mass_blocks": gaussian(part_splits[2], (NBLOCKS, SLOTS, BLOCK, BLOCK), (SLOTS * BLOCK) ** -0.5, 0.125, ((0, 8),)),
        "block_cols": draw_block_cols(jax.random.fold_in(jax.random.fold_in(splits[5], part), 71), part),
        "sources": gaussian(part_splits[4], (ORDER, COLUMNS), ORDER ** -0.5, 0.0625, ((0, 8),)),
    }


def reference(solutions, point_of_slot, mass_blocks, block_cols, sources):
    theta = 2.0 * math.pi * (point_of_slot.astype(jnp.float32) + 0.5) / POINTS
    powers = jnp.arange(1, MOMENTS + 1, dtype=jnp.float32)
    angles = powers[:, None] * theta[None, :]
    cosine = (jnp.cos(angles) / POINTS).astype(jnp.bfloat16)
    sine = (jnp.sin(angles) / POINTS).astype(jnp.bfloat16)
    real_part = solutions[:, :, :COLUMNS]
    imag_part = solutions[:, :, COLUMNS:]
    total = jnp.zeros((MOMENTS, ORDER, 2 * COLUMNS), jnp.float32)
    for group_index in range(N_QUAD):
        first = group_index * POINTS_DEV
        real_rows = real_part[first:first + POINTS_DEV].reshape(POINTS_DEV, ORDER * COLUMNS)
        imag_rows = imag_part[first:first + POINTS_DEV].reshape(POINTS_DEV, ORDER * COLUMNS)
        cos_group = cosine[:, first:first + POINTS_DEV]
        sin_group = sine[:, first:first + POINTS_DEV]
        out_real = jnp.dot(cos_group, real_rows, preferred_element_type=jnp.float32) - jnp.dot(sin_group, imag_rows, preferred_element_type=jnp.float32)
        out_imag = jnp.dot(sin_group, real_rows, preferred_element_type=jnp.float32) + jnp.dot(cos_group, imag_rows, preferred_element_type=jnp.float32)
        partial_value = jnp.concatenate([out_real.reshape(MOMENTS, ORDER, COLUMNS), out_imag.reshape(MOMENTS, ORDER, COLUMNS)], axis=2)
        total = total + partial_value.astype(jnp.bfloat16).astype(jnp.float32)
    moments = total.astype(jnp.bfloat16)
    moment_blocks = moments.reshape(MOMENTS, NBLOCKS, BLOCK, 2 * COLUMNS)

    def add_slot(accum, slot_index):
        columns_now = block_cols[:, slot_index]
        tiles = lax.dynamic_index_in_dim(mass_blocks, slot_index, 1, keepdims=False)
        chosen = moment_blocks[:, columns_now]
        accum = accum + jnp.einsum("bij,mbjc->mbic", tiles.astype(jnp.float32), chosen.astype(jnp.float32))
        return accum, None

    start = jnp.zeros((MOMENTS, NBLOCKS, BLOCK, 2 * COLUMNS), jnp.float32)
    accum, _ = lax.scan(add_slot, start, jnp.arange(SLOTS, dtype=jnp.int32))
    mass_applied = accum.astype(jnp.bfloat16).reshape(MOMENTS, ORDER, 2 * COLUMNS)
    reduced = jnp.einsum("nl,mnc->mlc", sources.astype(jnp.float32), mass_applied.astype(jnp.float32))
    return mass_applied, reduced
```

```python
import functools
import math

import jax
import jax.numpy as jnp
from jax import lax
from jax.experimental import pallas as pl
from jax.experimental.pallas import tpu as pltpu
from jax.sharding import PartitionSpec as P

MOMENTS = 8
TILE = 16
WINDOW = 3
ROUNDS = 3
MESH = pl.DeviceIdType.MESH


def kernel(
    n, quads, span, owned, points, chunk_blocks, reduce_here,
    point_hbm, cols_hbm, sources_hbm, sol_hbm, mass_hbm,
    out_hbm, red_out,
    sol, mass, weight, own, theirs, received, out_buf, term, rs_buf, red,
    point_ref, cols_ref, cols_vec, sources, places, v, back_send, back_recv, cross_send, cross_recv, halves, *rest,
):
    panels = rest[:owned]
    (sol_sem, mass_sem, small_sem, out_sem, q_send, q_recv, x_send, x_recv, f_send, f_recv,
     v_send, v_recv, rs_send, rs_recv, ag_send, ag_recv, hello) = rest[owned:]
    me = lax.axis_index("rows")
    quad = lax.axis_index("quad")
    rows_here, lanes = sol.shape[1:]
    half = lanes // 2
    width = 2 * sources.shape[0]
    block = rows_here // span
    slots = mass.shape[1]
    chunks = span // chunk_blocks
    chunk_rows = chunk_blocks * block
    bf16, f32 = jnp.bfloat16, jnp.float32
    odd = lax.rem(me, 2)
    partner = me + 1 - 2 * odd
    onward = lax.rem(me + 2 - 4 * odd + n, n)
    behind = lax.rem(me - 2 + 4 * odd + n, n)
    sends_on = jnp.where(odd == 1, me - 2 >= 0, me + 2 < n)
    gets_on = jnp.where(odd == 1, me + 2 < n, me - 2 >= 0)
    there = 2 * span * odd
    here = 2 * span - there

    def sol_copy(c):
        rows = pl.ds(c * chunk_rows, chunk_rows)
        return pltpu.make_async_copy(sol_hbm.at[:, rows], sol.at[:, rows], sol_sem.at[c])

    halfway = span // 2
    mass_copies = [
        pltpu.make_async_copy(mass_hbm.at[rows], mass.at[rows], mass_sem.at[h])
        for h, rows in ((0, pl.ds(0, halfway)), (1, pl.ds(halfway, span - halfway)))
    ]
    point_copy = pltpu.make_async_copy(point_hbm, point_ref, small_sem.at[0])
    cols_copy = pltpu.make_async_copy(cols_hbm, cols_ref, small_sem.at[1])
    vec_copy = pltpu.make_async_copy(cols_hbm, cols_vec, small_sem.at[2])
    share = pl.ds(pl.multiple_of(quad * (width // 2), width // 2), width // 2)
    sources_copy = pltpu.make_async_copy(sources_hbm.at[share], sources, small_sem.at[3])
    point_copy.start()
    for c in range(chunks):
        sol_copy(c).start()
    for copy in (cols_copy, vec_copy, sources_copy, *mass_copies):
        copy.start()

    barrier = pltpu.get_barrier_semaphore()

    def greet(semaphore):
        pl.semaphore_signal(semaphore, inc=1, device_id={"rows": partner}, device_id_type=MESH)

        @pl.when(sends_on)
        def _():
            pl.semaphore_signal(semaphore, inc=1, device_id={"rows": onward}, device_id_type=MESH)

        @pl.when(gets_on)
        def _():
            pl.semaphore_signal(semaphore, inc=1, device_id={"rows": behind}, device_id_type=MESH)

    greeted = 1 + sends_on.astype(jnp.int32) + gets_on.astype(jnp.int32)
    pl.semaphore_signal(barrier, inc=1, device_id={"quad": 1 - quad}, device_id_type=MESH)
    greet(barrier)

    part = lax.broadcasted_iota(jnp.int32, (2 * 2 * owned * TILE, 2 * 2 * owned), 0)
    spread = jnp.where(
        part // TILE == lax.broadcasted_iota(jnp.int32, part.shape, 1), 1.0, 0.0
    ).astype(bf16)
    across = lax.broadcasted_iota(jnp.int32, (points * TILE, points), 0)
    spread_points = jnp.where(
        across // TILE == lax.broadcasted_iota(jnp.int32, across.shape, 1), 1.0, 0.0
    ).astype(bf16)
    same = lax.rem(lax.broadcasted_iota(jnp.int32, (part.shape[0], across.shape[0]), 0), TILE) == lax.rem(
        lax.broadcasted_iota(jnp.int32, (part.shape[0], across.shape[0]), 1), TILE
    )
    total_points = points * quads
    shape = (2 * MOMENTS, points)
    row = lax.broadcasted_iota(jnp.int32, shape, 0)
    lane = lax.broadcasted_iota(jnp.int32, shape, 1)
    moment = lax.rem(row + owned * quad, MOMENTS) + 1
    point_copy.wait()
    point = jnp.zeros(shape, jnp.int32)
    for s in range(points):
        point = jnp.where(lane == s, point_ref[s], point)
    turn = lax.rem((2 * point + 1) * moment, 2 * total_points)
    turn = jnp.where(turn >= total_points, turn - 2 * total_points, turn)
    angle = turn.astype(f32) * (math.pi / total_points)
    trig = (jnp.where(row < MOMENTS, jnp.cos(angle), jnp.sin(angle)) / total_points).astype(bf16)
    tall = jnp.dot(spread, trig, preferred_element_type=f32).astype(bf16)
    wide = lax.dot_general(tall, spread_points, (((1,), (1,)), ((), ())), preferred_element_type=f32)
    weight[...] = jnp.where(same, wide, 0.0).astype(bf16)

    def quad_copy(c):
        rows = pl.ds(c * chunk_rows, chunk_rows)
        return pltpu.make_async_remote_copy(
            src_ref=theirs.at[:, rows], dst_ref=received.at[:, rows],
            send_sem=q_send.at[c], recv_sem=q_recv.at[c],
            device_id={"quad": 1 - quad}, device_id_type=MESH,
        )

    order = [(k, c) for k in range(owned) for c in range(chunks)]
    pieces = len(order)

    def at(q, base):
        k, c = order[q]
        return panels[k].at[pl.ds(base + c * chunk_blocks, chunk_blocks)]

    def cross(q, base):
        return pltpu.make_async_remote_copy(
            src_ref=at(q, span), dst_ref=at(q, base),
            send_sem=x_send.at[q], recv_sem=x_recv.at[q],
            device_id={"rows": partner}, device_id_type=MESH,
        )

    def forward(q, base):
        return pltpu.make_async_remote_copy(
            src_ref=at(q, here), dst_ref=at(q, base),
            send_sem=f_send.at[q], recv_sem=f_recv.at[q],
            device_id={"rows": onward}, device_id_type=MESH,
        )

    def relay(q):
        cross(q, there).wait_send()
        if q + WINDOW < pieces:
            cross(q + WINDOW, there).start()
        cross(q, here).wait_recv()

        @pl.when(sends_on)
        def _():
            forward(q, there).start()

    def arrived(k):
        @pl.when(gets_on)
        def _():
            for p in range(chunks):
                forward(order.index((k, p)), there).wait_recv()

    def weigh(c):
        for g in range(chunk_rows // (2 * TILE)):
            first = c * chunk_rows + g * 2 * TILE
            second = first + TILE
            stacked = jnp.concatenate(
                [
                    sol[:, pl.ds(first, TILE), :].reshape(points * TILE, lanes),
                    sol[:, pl.ds(second, TILE), :].reshape(points * TILE, lanes),
                ],
                axis=1,
            )
            z = jnp.dot(weight[...], stacked, preferred_element_type=f32)
            height = 2 * owned * TILE
            negative = lax.broadcasted_iota(jnp.int32, (height, lanes), 1) < half
            for h, start in ((0, first), (1, second)):
                straight = z[:height, h * lanes:(h + 1) * lanes]
                crossed = pltpu.roll(z[height:, h * lanes:(h + 1) * lanes], half, 1)
                value = straight + jnp.where(negative, -crossed, crossed)
                value = value.astype(bf16).reshape(2 * owned, TILE, lanes)
                own[:, pl.ds(start, TILE), :] = value[:owned]
                theirs[:, pl.ds(start, TILE), :] = value[owned:]

    def add_up(c):
        quad_copy(c).wait_recv()
        for k in range(owned):
            for b in range(c * chunk_blocks, (c + 1) * chunk_blocks):
                rows = pl.ds(b * block, block)
                total = own[k, rows, :].astype(f32) + received[k, rows, :].astype(f32)
                panels[k][span + b] = total.astype(bf16)
        if c < WINDOW:
            cross(order.index((0, c)), there).start()

    for c in range(chunks):
        sol_copy(c).wait()
        weigh(c)
        if c == 0:
            pl.semaphore_wait(barrier, 1 + greeted)
        quad_copy(c).start()
        if c > 0:
            add_up(c - 1)
    add_up(chunks - 1)
    offset = (me - 1) * span

    def say_hello(r):
        if reduce_here:
            greet(hello.at[r])

    def hear_hello(r):
        if reduce_here:
            pl.semaphore_wait(hello.at[r], greeted)

    reach = 2 * span + 1
    tall_rows, wide_cols = reach * TILE, slots * TILE

    def prepare_places():
        vec_copy.wait()
        local_cols = (cols_vec[...] - offset).astype(f32)
        local_cols = local_cols - lax.broadcasted_iota(jnp.int32, local_cols.shape, 0).astype(f32)
        copies = jnp.where(
            lax.broadcasted_iota(jnp.int32, (slots, wide_cols), 1) // TILE
            == lax.broadcasted_iota(jnp.int32, (slots, wide_cols), 0), 1.0, 0.0
        ).astype(bf16)
        places[...] = jnp.dot(local_cols.astype(bf16), copies, preferred_element_type=f32)
        v[...] = jnp.zeros_like(v)

    def project(first, last):
        ra = lax.broadcasted_iota(jnp.int32, (tall_rows, wide_cols), 0)
        ca = lax.broadcasted_iota(jnp.int32, (tall_rows, wide_cols), 1)
        diagonal = lax.rem(ra, TILE) == lax.rem(ca, TILE)
        column = (ra // TILE).astype(f32)

        def one(i):
            rows = jnp.concatenate([mass[i, j] for j in range(slots)], axis=1)
            left = sources[:, pl.ds(pl.multiple_of(i * block, block), block)]
            product = jnp.dot(left, rows, preferred_element_type=f32).astype(bf16)
            tiles = width // 2 // TILE
            stacked = jnp.concatenate(
                [
                    jnp.concatenate(
                        [product[t * TILE:(t + 1) * TILE, j * block:(j + 1) * block] for t in range(tiles)], axis=1
                    )
                    for j in range(slots)
                ],
                axis=0,
            )
            chosen = jnp.where(diagonal & (column == places[pl.ds(i, 1), :]), 1.0, 0.0).astype(bf16)
            summed = jnp.dot(chosen, stacked, preferred_element_type=f32)
            for t in range(tiles):
                v[pl.ds(i, reach), t * TILE:(t + 1) * TILE, :] += summed[:, t * block:(t + 1) * block].reshape(
                    reach, TILE, block
                )

        def body(i, carry):
            one(first + i)
            return carry

        lax.fori_loop(0, last - first, body, 0, unroll=True)

    def back_copy():
        return pltpu.make_async_remote_copy(
            src_ref=back_send, dst_ref=back_recv, send_sem=v_send.at[0], recv_sem=v_recv.at[0],
            device_id={"rows": behind}, device_id_type=MESH,
        )

    def cross_copy():
        return pltpu.make_async_remote_copy(
            src_ref=cross_send, dst_ref=cross_recv, send_sem=v_send.at[1], recv_sem=v_recv.at[1],
            device_id={"rows": partner}, device_id_type=MESH,
        )

    def halves_copy(which):
        return pltpu.make_async_remote_copy(
            src_ref=halves.at[which], dst_ref=halves.at[which], send_sem=v_send.at[2], recv_sem=v_recv.at[2],
            device_id={"quad": 1 - quad}, device_id_type=MESH,
        )

    def send_back():
        @pl.when(gets_on)
        def _():
            back_send[...] = v[pl.ds(there, span)].astype(bf16)
            back_copy().start()

    def send_across():
        @pl.when(sends_on)
        def _():
            back_copy().wait_recv()
            cross_send[...] = (v[pl.ds(here, span)] + back_recv[...].astype(f32)).astype(bf16)

        @pl.when(jnp.logical_not(sends_on))
        def _():
            cross_send[...] = v[pl.ds(here, span)].astype(bf16)

        cross_copy().start()

    def share_halves():
        cross_copy().wait_recv()
        halves[quad] = v[span:2 * span] + cross_recv[...].astype(f32)
        halves_copy(quad).start()

    def rs_copy(o):
        return pltpu.make_async_remote_copy(
            src_ref=term.at[:, lax.rem(me + o, n)], dst_ref=rs_buf.at[:, o],
            send_sem=rs_send.at[o], recv_sem=rs_recv.at[o],
            device_id={"rows": lax.rem(me + o, n)}, device_id_type=MESH,
        )

    def ag_copy(o, origin):
        return pltpu.make_async_remote_copy(
            src_ref=red.at[:, origin], dst_ref=red.at[:, origin],
            send_sem=ag_send.at[o], recv_sem=ag_recv.at[o],
            device_id={"rows": lax.rem(me + o, n)}, device_id_type=MESH,
        )

    def make_terms():
        halves_copy(1 - quad).wait_recv()
        left = jnp.concatenate(
            [jnp.concatenate([halves[h, b] for b in range(span)], axis=1) for h in range(2)], axis=0
        ).astype(bf16)
        for k in range(owned):
            right = panels[k][span:2 * span].reshape(rows_here, lanes)
            value = jnp.dot(left, right, preferred_element_type=f32)
            if reduce_here:
                term[k] = value.reshape(term.shape[1:])
            else:
                red_out[k] = value
        if reduce_here:
            for o in range(1, n):
                rs_copy(o).start()

    def reduce():
        if not reduce_here:
            return
        total = term[:, me]
        for o in range(1, n):
            rs_copy(o).wait_recv()
            total = total + rs_buf[:, o]
        red[:, me] = total
        for o in range(1, n):
            ag_copy(o, me).start()

    def apply_mass(k, first, last):
        panel = panels[k]

        def block_row(i):
            left_side = jnp.concatenate([mass[i, j] for j in range(slots)], axis=1)
            right_side = jnp.concatenate(
                [panel[jnp.clip(cols_ref[i, j] - offset, 0, 3 * span - 1)] for j in range(slots)],
                axis=0,
            )
            value = jnp.dot(left_side, right_side, preferred_element_type=f32)
            out_buf[k, pl.ds(pl.multiple_of(i * block, block), block), :] = value.astype(bf16)

        def body(i, carry):
            block_row(first + i)
            return carry

        lax.fori_loop(0, last - first, body, 0, unroll=True)

    def out_copy(k):
        return pltpu.make_async_copy(out_buf.at[k], out_hbm.at[k], out_sem.at[k])

    steps = [lambda k=k, h=h: apply_mass(k, (0, halfway)[h], (halfway, span)[h]) for k in range(owned) for h in range(2)]

    def finish(k):
        out_copy(k).start()

    prepare_places()
    say_hello(0)
    mass_copies[0].wait()
    sources_copy.wait()
    project(0, halfway)
    relay(0)
    relay(1)
    mass_copies[1].wait()
    project(halfway, span)
    send_back()
    relay(2)
    relay(3)
    hear_hello(0)
    say_hello(1)
    cols_copy.wait()
    relay(4)
    send_across()
    relay(5)
    arrived(0)
    steps[0]()
    relay(6)
    relay(7)
    steps[1]()
    finish(0)
    hear_hello(1)
    say_hello(2)
    relay(8)
    share_halves()
    relay(9)
    hear_hello(2)
    make_terms()
    relay(10)
    arrived(1)
    steps[2]()
    relay(11)
    relay(12)
    steps[3]()
    finish(1)
    relay(13)
    relay(14)
    reduce()
    relay(15)
    arrived(2)
    steps[4]()
    relay(16)
    steps[5]()
    finish(2)
    for q in range(17, pieces):
        relay(q)
    arrived(3)
    steps[6]()
    steps[7]()
    finish(3)

    @pl.when(sends_on)
    def _():
        for q in range(pieces):
            forward(q, there).wait_send()

    @pl.when(gets_on)
    def _():
        back_copy().wait_send()

    cross_copy().wait_send()
    halves_copy(quad).wait_send()
    for c in range(chunks):
        quad_copy(c).wait_send()
    if reduce_here:
        for o in range(1, n):
            rs_copy(o).wait_send()
            ag_copy(o, me).wait_send()
            ag_copy(o, lax.rem(me + n - o, n)).wait_recv()
        for k in range(owned):
            red_out[k] = red[k].reshape(red_out.shape[1:])
    for k in range(owned):
        out_copy(k).wait()


def local(n, quads, solutions, point_of_slot, mass_blocks, block_cols, sources):
    points, rows_here, lanes = solutions.shape
    width = lanes // 2
    span, slots, block_size = mass_blocks.shape[:3]
    owned = MOMENTS // quads
    chunk_blocks = 2
    chunks = span // chunk_blocks
    reduce_here = n <= 8 and width % n == 0
    parts = n if reduce_here else 1
    bf16, f32 = jnp.bfloat16, jnp.float32
    dma = pltpu.SemaphoreType.DMA
    pieces = chunks * owned
    vmem = pl.BlockSpec(memory_space=pltpu.VMEM)
    hbm = pl.BlockSpec(memory_space=pl.ANY)
    mass_applied, reduced = pl.pallas_call(
        functools.partial(kernel, n, quads, span, owned, points, chunk_blocks, reduce_here),
        out_shape=(
            jax.ShapeDtypeStruct((owned, rows_here, lanes), bf16),
            jax.ShapeDtypeStruct((owned, width, lanes), f32),
        ),
        in_specs=[hbm] * 5,
        out_specs=(hbm, vmem),
        scratch_shapes=[
            pltpu.VMEM(solutions.shape, bf16),
            pltpu.VMEM(mass_blocks.shape, bf16),
            pltpu.VMEM((2 * MOMENTS * TILE, points * TILE), bf16),
            pltpu.VMEM((owned, rows_here, lanes), bf16),
            pltpu.VMEM((owned, rows_here, lanes), bf16),
            pltpu.VMEM((owned, rows_here, lanes), bf16),
            pltpu.VMEM((owned, rows_here, lanes), bf16),
            pltpu.VMEM((owned, parts, width // parts, lanes), f32),
            pltpu.VMEM((owned, parts, width // parts, lanes), f32),
            pltpu.VMEM((owned, parts, width // parts, lanes), f32),
            pltpu.SMEM(point_of_slot.shape, jnp.int32),
            pltpu.SMEM(block_cols.shape, jnp.int32),
            pltpu.VMEM(block_cols.shape, jnp.int32),
            pltpu.VMEM((width // 2, rows_here), bf16),
            pltpu.VMEM((span, slots * TILE), f32),
            pltpu.VMEM((3 * span, width // 2, block_size), f32),
            pltpu.VMEM((span, width // 2, block_size), bf16),
            pltpu.VMEM((span, width // 2, block_size), bf16),
            pltpu.VMEM((span, width // 2, block_size), bf16),
            pltpu.VMEM((span, width // 2, block_size), bf16),
            pltpu.VMEM((2, span, width // 2, block_size), f32),
        ]
        + [pltpu.VMEM((3 * span, block_size, lanes), bf16) for _ in range(owned)]
        + [
            dma((chunks,)), dma((2,)), dma((4,)), dma((owned,)), dma((chunks,)), dma((chunks,)),
            dma((pieces,)), dma((pieces,)), dma((pieces,)), dma((pieces,)), dma((3,)), dma((3,)),
            dma((parts,)), dma((parts,)), dma((parts,)), dma((parts,)), pltpu.SemaphoreType.REGULAR((ROUNDS,)),
        ],
        compiler_params=pltpu.CompilerParams(
            collective_id=0, has_side_effects=True, vmem_limit_bytes=48 * 1024 * 1024
        ),
    )(point_of_slot, block_cols, sources.T, solutions, mass_blocks)
    if not reduce_here:
        reduced = lax.psum(reduced, "rows")
    return mass_applied, reduced


def solution(mesh):
    in_specs = (
        P("quad", ("group", "rows"), None),
        P(("group", "quad")),
        P(("group", "rows"), None, None, None),
        P(("group", "rows"), None),
        P(("group", "rows"), None),
    )
    out_specs = (P("quad", ("group", "rows"), None), P(("group", "quad"), None, None))
    step = functools.partial(local, mesh.shape["rows"], mesh.shape["quad"])
    return jax.shard_map(step, mesh=mesh, in_specs=in_specs, out_specs=out_specs, check_vma=False)
```

```python
import contextlib
import functools
import math

import jax
import jax.numpy as jnp
from jax import lax
from jax.experimental import pallas as pl
from jax.experimental.pallas import tpu as pltpu
from jax.sharding import PartitionSpec as P

MOMENTS = 8
TILE = 16
WINDOW = 6
LAST_WINDOW = 4
LATE = 5
ROUNDS = 2
NAMED = False
RS_TYPE = jnp.bfloat16
AG_TYPE = jnp.bfloat16
MESH = pl.DeviceIdType.MESH


def part_of(name):
    return jax.named_scope(name) if NAMED else contextlib.nullcontext()


def kernel(
    n, quads, span, owned, points, chunk_blocks, reduce_here,
    point_hbm, cols_hbm, sources_hbm, sol_hbm, mass_hbm,
    out_hbm, red_out,
    sol, mass, weight, own, theirs, received, out_buf, term, rs_send_buf, rs_buf, pair_send, pair_recv, red, late,
    point_ref, cols_ref, cols_vec, sources, places, v, back_send, back_recv, cross_send, cross_recv, halves, *rest,
):
    panels = rest[:owned]
    (sol_sem, mass_sem, small_sem, out_sem, q_send, q_recv, x_send, x_recv, f_send, f_recv,
     v_send, v_recv, rs_send, rs_recv, pair_sem, ag_send, ag_recv, hello) = rest[owned:]
    me = lax.axis_index("rows")
    quad = lax.axis_index("quad")
    rows_here, lanes = sol.shape[1:]
    half = lanes // 2
    width = 2 * sources.shape[0]
    block = rows_here // span
    slots = mass.shape[1]
    chunks = span // chunk_blocks
    chunk_rows = chunk_blocks * block
    bf16, f32 = jnp.bfloat16, jnp.float32
    odd = lax.rem(me, 2)
    partner = me + 1 - 2 * odd
    onward = lax.rem(me + 2 - 4 * odd + n, n)
    behind = lax.rem(me - 2 + 4 * odd + n, n)
    sends_on = jnp.where(odd == 1, me - 2 >= 0, me + 2 < n)
    gets_on = jnp.where(odd == 1, me + 2 < n, me - 2 >= 0)
    there = 2 * span * odd
    here = 2 * span - there

    def sol_copy(c):
        rows = pl.ds(c * chunk_rows, chunk_rows)
        return pltpu.make_async_copy(sol_hbm.at[:, rows], sol.at[:, rows], sol_sem.at[c])

    halfway = span // 2
    mass_copies = [
        pltpu.make_async_copy(mass_hbm.at[rows], mass.at[rows], mass_sem.at[h])
        for h, rows in ((0, pl.ds(0, halfway)), (1, pl.ds(halfway, span - halfway)))
    ]
    point_copy = pltpu.make_async_copy(point_hbm, point_ref, small_sem.at[0])
    cols_copy = pltpu.make_async_copy(cols_hbm, cols_ref, small_sem.at[1])
    vec_copy = pltpu.make_async_copy(cols_hbm, cols_vec, small_sem.at[2])
    share = pl.ds(pl.multiple_of(quad * (width // 2), width // 2), width // 2)
    sources_copy = pltpu.make_async_copy(sources_hbm.at[share], sources, small_sem.at[3])
    point_copy.start()
    queue = [sol_copy(c) for c in range(chunks)] + [cols_copy, vec_copy, sources_copy, *mass_copies]
    for copy in queue[:2]:
        copy.start()

    barrier = pltpu.get_barrier_semaphore()

    def greet(semaphore):
        pl.semaphore_signal(semaphore, inc=1, device_id={"rows": partner}, device_id_type=MESH)

        @pl.when(sends_on)
        def _():
            pl.semaphore_signal(semaphore, inc=1, device_id={"rows": onward}, device_id_type=MESH)

        @pl.when(gets_on)
        def _():
            pl.semaphore_signal(semaphore, inc=1, device_id={"rows": behind}, device_id_type=MESH)

    greeted = 1 + sends_on.astype(jnp.int32) + gets_on.astype(jnp.int32)
    pl.semaphore_signal(barrier, inc=1, device_id={"quad": 1 - quad}, device_id_type=MESH)
    greet(barrier)

    part = lax.broadcasted_iota(jnp.int32, (2 * 2 * owned * TILE, 2 * 2 * owned), 0)
    spread = jnp.where(
        part // TILE == lax.broadcasted_iota(jnp.int32, part.shape, 1), 1.0, 0.0
    ).astype(bf16)
    across = lax.broadcasted_iota(jnp.int32, (points * TILE, points), 0)
    spread_points = jnp.where(
        across // TILE == lax.broadcasted_iota(jnp.int32, across.shape, 1), 1.0, 0.0
    ).astype(bf16)
    same = lax.rem(lax.broadcasted_iota(jnp.int32, (part.shape[0], across.shape[0]), 0), TILE) == lax.rem(
        lax.broadcasted_iota(jnp.int32, (part.shape[0], across.shape[0]), 1), TILE
    )
    total_points = points * quads
    shape = (2 * MOMENTS, points)
    row = lax.broadcasted_iota(jnp.int32, shape, 0)
    lane = lax.broadcasted_iota(jnp.int32, shape, 1)
    moment = lax.rem(row + owned * quad, MOMENTS) + 1
    point_copy.wait()
    point = jnp.zeros(shape, jnp.int32)
    for s in range(points):
        point = jnp.where(lane == s, point_ref[s], point)
    turn = lax.rem((2 * point + 1) * moment, 2 * total_points)
    turn = jnp.where(turn >= total_points, turn - 2 * total_points, turn)
    angle = turn.astype(f32) * (math.pi / total_points)
    trig = (jnp.where(row < MOMENTS, jnp.cos(angle), jnp.sin(angle)) / total_points).astype(bf16)
    tall = jnp.dot(spread, trig, preferred_element_type=f32).astype(bf16)
    wide = lax.dot_general(tall, spread_points, (((1,), (1,)), ((), ())), preferred_element_type=f32)
    weight[...] = jnp.where(same, wide, 0.0).astype(bf16)

    def quad_copy(c):
        rows = pl.ds(c * chunk_rows, chunk_rows)
        return pltpu.make_async_remote_copy(
            src_ref=theirs.at[:, rows], dst_ref=received.at[:, rows],
            send_sem=q_send.at[c], recv_sem=q_recv.at[c],
            device_id={"quad": 1 - quad}, device_id_type=MESH,
        )

    last = owned - 1
    order = [(k, c * chunk_blocks, chunk_blocks) for k in range(last) for c in range(chunks)]
    order += [(last, b, 1) for b in range(span)]
    pieces = len(order)
    starts = [[] for _ in range(pieces)]
    begun, sent_blocks = 2, [sum(count for _, _, count in order[:q + 1]) for q in range(pieces)]
    for q in range(pieces):
        while begun < pieces:
            limit = WINDOW if order[begun][0] < last else LAST_WINDOW
            if sent_blocks[begun] - sent_blocks[q] > limit:
                break
            starts[q].append(begun)
            begun += 1

    def blocks_of(q, parity):
        k, first, count = order[q]
        if k == last:
            first = first + parity * (span - count - 2 * first)
        return first, count

    def at(q, base, parity):
        first, count = blocks_of(q, parity)
        return panels[order[q][0]].at[pl.ds(base + first, count)]

    def cross(q, base):
        return pltpu.make_async_remote_copy(
            src_ref=at(q, span, odd), dst_ref=at(q, base, odd),
            send_sem=x_send.at[q], recv_sem=x_recv.at[q],
            device_id={"rows": partner}, device_id_type=MESH,
        )

    def forward(q):
        k, first, count = order[q]
        if k == last and first >= span - LATE:
            target = late.at[pl.ds(first - (span - LATE), count)]
        else:
            target = at(q, there, 1 - odd)
        return pltpu.make_async_remote_copy(
            src_ref=at(q, here, 1 - odd), dst_ref=target,
            send_sem=f_send.at[q], recv_sem=f_recv.at[q],
            device_id={"rows": onward}, device_id_type=MESH,
        )

    def relay(q):
        with part_of(f"relay_{q}_sent"):
            cross(q, there).wait_send()
            for p in starts[q]:
                cross(p, there).start()
        with part_of(f"relay_{q}_here"):
            cross(q, here).wait_recv()

        @pl.when(sends_on)
        def _():
            forward(q).start()

    def arrived(k, first=0, stop=None):
        with part_of(f"arrived_{k}"):

            @pl.when(gets_on)
            def _():
                for q in range(pieces):
                    if order[q][0] == k and first <= order[q][1] < (span if stop is None else stop):
                        forward(q).wait_recv()

    def place_late():
        @pl.when(gets_on)
        def _():
            for q in range(pieces):
                if order[q][0] == last and order[q][1] >= span - LATE:
                    first, count = blocks_of(q, 1 - odd)
                    panels[last][pl.ds(there + first, count)] = late[
                        pl.ds(order[q][1] - (span - LATE), count)
                    ]

    def weigh(c):
        for g in range(chunk_rows // (2 * TILE)):
            first = c * chunk_rows + g * 2 * TILE
            second = first + TILE
            stacked = jnp.concatenate(
                [
                    sol[:, pl.ds(first, TILE), :].reshape(points * TILE, lanes),
                    sol[:, pl.ds(second, TILE), :].reshape(points * TILE, lanes),
                ],
                axis=1,
            )
            z = jnp.dot(weight[...], stacked, preferred_element_type=f32)
            height = 2 * owned * TILE
            negative = lax.broadcasted_iota(jnp.int32, (height, lanes), 1) < half
            for h, start in ((0, first), (1, second)):
                straight = z[:height, h * lanes:(h + 1) * lanes]
                crossed = pltpu.roll(z[height:, h * lanes:(h + 1) * lanes], half, 1)
                value = straight + jnp.where(negative, -crossed, crossed)
                value = value.astype(bf16).reshape(2 * owned, TILE, lanes)
                own[:, pl.ds(start, TILE), :] = value[:owned]
                theirs[:, pl.ds(start, TILE), :] = value[owned:]

    def add_up(c):
        quad_copy(c).wait_recv()
        for k in range(owned):
            for b in range(c * chunk_blocks, (c + 1) * chunk_blocks):
                rows = pl.ds(b * block, block)
                total = own[k, rows, :].astype(f32) + received[k, rows, :].astype(f32)
                panels[k][span + b] = total.astype(bf16)
        if c < 2:
            cross(c, there).start()

    for c in range(chunks):
        with part_of(f"load_{c}"):
            sol_copy(c).wait()
            for copy in queue[2 + c:3 + c] if c < chunks - 2 else queue[chunks + (0, 4)[c - chunks + 2]:][:(4, 1)[c - chunks + 2]]:
                copy.start()
        with part_of(f"weigh_{c}"):
            weigh(c)
        if c == 0:
            with part_of("meet"):
                pl.semaphore_wait(barrier, 1 + greeted)
        quad_copy(c).start()
        if c > 0:
            with part_of(f"add_{c}"):
                add_up(c - 1)
    with part_of("add_last"):
        add_up(chunks - 1)
    offset = (me - 1) * span

    def say_hello(r):
        if reduce_here:
            greet(hello.at[r])

    def hear_hello(r):
        if reduce_here:
            pl.semaphore_wait(hello.at[r], greeted)

    reach = 2 * span + 1
    tall_rows, wide_cols = reach * TILE, slots * TILE

    def prepare_places():
        vec_copy.wait()
        local_cols = (cols_vec[...] - offset).astype(f32)
        local_cols = local_cols - lax.broadcasted_iota(jnp.int32, local_cols.shape, 0).astype(f32)
        copies = jnp.where(
            lax.broadcasted_iota(jnp.int32, (slots, wide_cols), 1) // TILE
            == lax.broadcasted_iota(jnp.int32, (slots, wide_cols), 0), 1.0, 0.0
        ).astype(bf16)
        places[...] = jnp.dot(local_cols.astype(bf16), copies, preferred_element_type=f32)
        v[...] = jnp.zeros_like(v)

    def project(first, last):
        ra = lax.broadcasted_iota(jnp.int32, (tall_rows, wide_cols), 0)
        ca = lax.broadcasted_iota(jnp.int32, (tall_rows, wide_cols), 1)
        diagonal = lax.rem(ra, TILE) == lax.rem(ca, TILE)
        column = (ra // TILE).astype(f32)

        def one(i):
            rows = jnp.concatenate([mass[i, j] for j in range(slots)], axis=1)
            left = sources[:, pl.ds(pl.multiple_of(i * block, block), block)]
            product = jnp.dot(left, rows, preferred_element_type=f32).astype(bf16)
            tiles = width // 2 // TILE
            stacked = jnp.concatenate(
                [
                    jnp.concatenate(
                        [product[t * TILE:(t + 1) * TILE, j * block:(j + 1) * block] for t in range(tiles)], axis=1
                    )
                    for j in range(slots)
                ],
                axis=0,
            )
            chosen = jnp.where(diagonal & (column == places[pl.ds(i, 1), :]), 1.0, 0.0).astype(bf16)
            summed = jnp.dot(chosen, stacked, preferred_element_type=f32)
            for t in range(tiles):
                v[pl.ds(i, reach), t * TILE:(t + 1) * TILE, :] += summed[:, t * block:(t + 1) * block].reshape(
                    reach, TILE, block
                )

        def body(i, carry):
            one(first + i)
            return carry

        lax.fori_loop(0, last - first, body, 0, unroll=True)

    def back_copy():
        return pltpu.make_async_remote_copy(
            src_ref=back_send, dst_ref=back_recv, send_sem=v_send.at[0], recv_sem=v_recv.at[0],
            device_id={"rows": behind}, device_id_type=MESH,
        )

    def cross_copy():
        return pltpu.make_async_remote_copy(
            src_ref=cross_send, dst_ref=cross_recv, send_sem=v_send.at[1], recv_sem=v_recv.at[1],
            device_id={"rows": partner}, device_id_type=MESH,
        )

    def halves_copy(which):
        return pltpu.make_async_remote_copy(
            src_ref=halves.at[which], dst_ref=halves.at[which], send_sem=v_send.at[2], recv_sem=v_recv.at[2],
            device_id={"quad": 1 - quad}, device_id_type=MESH,
        )

    def send_back():
        @pl.when(gets_on)
        def _():
            back_send[...] = v[pl.ds(there, span)].astype(bf16)
            back_copy().start()

    def send_across():
        @pl.when(sends_on)
        def _():
            back_copy().wait_recv()
            cross_send[...] = (v[pl.ds(here, span)] + back_recv[...].astype(f32)).astype(bf16)

        @pl.when(jnp.logical_not(sends_on))
        def _():
            cross_send[...] = v[pl.ds(here, span)].astype(bf16)

        cross_copy().start()

    def share_halves():
        cross_copy().wait_recv()
        halves[quad] = v[span:2 * span] + cross_recv[...].astype(f32)
        halves_copy(quad).start()

    layer, layers = me // 2, n // 2

    def rs_copy(o):
        return pltpu.make_async_remote_copy(
            src_ref=rs_send_buf.at[lax.rem(layer + o, layers)], dst_ref=rs_buf.at[o],
            send_sem=rs_send.at[o], recv_sem=rs_recv.at[o],
            device_id={"rows": 2 * lax.rem(layer + o, layers) + odd}, device_id_type=MESH,
        )

    def pair_copy():
        return pltpu.make_async_remote_copy(
            src_ref=pair_send, dst_ref=pair_recv, send_sem=pair_sem.at[0], recv_sem=pair_sem.at[1],
            device_id={"rows": partner}, device_id_type=MESH,
        )

    def ag_copy(o, origin):
        return pltpu.make_async_remote_copy(
            src_ref=red.at[origin], dst_ref=red.at[origin],
            send_sem=ag_send.at[o], recv_sem=ag_recv.at[o],
            device_id={"rows": 2 * lax.rem(layer + o, layers) + odd}, device_id_type=MESH,
        )

    def make_terms():
        halves_copy(1 - quad).wait_recv()
        left = jnp.concatenate(
            [jnp.concatenate([halves[h, b] for b in range(span)], axis=1) for h in range(2)], axis=0
        )
        high = left.astype(bf16)
        low = (left - high.astype(f32)).astype(bf16)
        both = jnp.concatenate([high, low], axis=0)
        for k in range(owned):
            right = panels[k][span:2 * span].reshape(rows_here, lanes)
            value = jnp.dot(both, right, preferred_element_type=f32)
            value = value[:width] + value[width:]
            if reduce_here:
                value = value.reshape(layers, width // layers, lanes)
                term[:, k] = value
                rs_send_buf[:, k] = value.astype(rs_send_buf.dtype)
            else:
                red_out[k] = value
        if reduce_here:
            for o in range(1, layers):
                rs_copy(o).start()

    def reduce():
        if reduce_here:
            total = term[layer]
            for o in range(1, layers):
                rs_copy(o).wait_recv()
                total = total + rs_buf[o].astype(f32)
            pair_send[...] = total
            pair_copy().start()

    def spread_total():
        if reduce_here:
            pair_copy().wait_recv()
            red[layer] = (pair_send[...] + pair_recv[...]).astype(red.dtype)
            for o in range(1, layers):
                ag_copy(o, layer).start()

    def apply_mass(k, begin, end):
        panel = panels[k]

        def block_row(i):
            left_side = jnp.concatenate([mass[i, j] for j in range(slots)], axis=1)
            right_side = jnp.concatenate(
                [panel[jnp.clip(cols_ref[i, j] - offset, 0, 3 * span - 1)] for j in range(slots)],
                axis=0,
            )
            value = jnp.dot(left_side, right_side, preferred_element_type=f32)
            out_buf[k, pl.ds(pl.multiple_of(i * block, block), block), :] = value.astype(bf16)

        def body(i, carry):
            block_row(jnp.where(odd == 1, begin + i, span - 1 - begin - i))
            return carry

        with part_of(f"mass_{k}"):
            lax.fori_loop(0, end - begin, body, 0, unroll=True)

    def out_copy(k):
        return pltpu.make_async_copy(out_buf.at[k], out_hbm.at[k], out_sem.at[k])

    def finish(k):
        out_copy(k).start()

    prepare_places()
    say_hello(0)
    mass_copies[0].wait()
    sources_copy.wait()
    with part_of("project"):
        project(0, 3)
    relay(0)
    with part_of("project"):
        project(3, 5)
    mass_copies[1].wait()
    relay(1)
    with part_of("project"):
        project(5, 8)
    relay(2)
    with part_of("project"):
        project(8, span)
        send_back()
    cols_copy.wait()
    relay(3)
    relay(4)
    hear_hello(0)
    say_hello(1)
    with part_of("send_across"):
        send_across()
    relay(5)
    relay(6)
    arrived(0)
    apply_mass(0, 0, halfway)
    relay(7)
    apply_mass(0, halfway, span)
    finish(0)
    relay(8)
    with part_of("share_halves"):
        share_halves()
    relay(9)
    hear_hello(1)
    relay(10)
    with part_of("terms"):
        make_terms()
    relay(11)
    arrived(1)
    apply_mass(1, 0, halfway)
    relay(12)
    with part_of("reduce"):
        reduce()
    relay(13)
    apply_mass(1, halfway, span)
    finish(1)
    relay(14)
    with part_of("reduce"):
        spread_total()
    relay(15)
    relay(16)
    relay(17)
    relay(18)
    arrived(2)
    apply_mass(2, 0, halfway)
    relay(19)
    relay(20)
    apply_mass(2, halfway, span)
    finish(2)
    for q in range(21, pieces):
        relay(q)
    arrived(last, 0, span - LATE)
    apply_mass(last, 0, span - LATE)
    arrived(last, span - LATE)
    place_late()
    apply_mass(last, span - LATE, span)
    finish(last)

    with part_of("all_sent"):

        @pl.when(sends_on)
        def _():
            for q in range(pieces):
                forward(q).wait_send()

        @pl.when(gets_on)
        def _():
            back_copy().wait_send()

        cross_copy().wait_send()
        halves_copy(quad).wait_send()
        for c in range(chunks):
            quad_copy(c).wait_send()
    with part_of("gather"):
        if reduce_here:
            pair_copy().wait_send()
            for o in range(1, layers):
                rs_copy(o).wait_send()
                ag_copy(o, layer).wait_send()
                ag_copy(o, lax.rem(layer + layers - o, layers)).wait_recv()
            for k in range(owned):
                red_out[k] = red[:, k].astype(f32).reshape(red_out.shape[1:])
    with part_of("write"):
        for k in range(owned):
            out_copy(k).wait()


def local(n, quads, solutions, point_of_slot, mass_blocks, block_cols, sources):
    points, rows_here, lanes = solutions.shape
    width = lanes // 2
    span, slots, block_size = mass_blocks.shape[:3]
    owned = MOMENTS // quads
    chunk_blocks = 2
    chunks = span // chunk_blocks
    reduce_here = n <= 8 and width % (16 * n // 2) == 0
    parts = n // 2 if reduce_here else 1
    bf16, f32 = jnp.bfloat16, jnp.float32
    dma = pltpu.SemaphoreType.DMA
    pieces = chunks * (owned - 1) + span
    quarter = (parts, owned, width // parts, lanes)
    vmem = pl.BlockSpec(memory_space=pltpu.VMEM)
    hbm = pl.BlockSpec(memory_space=pl.ANY)
    mass_applied, reduced = pl.pallas_call(
        functools.partial(kernel, n, quads, span, owned, points, chunk_blocks, reduce_here),
        out_shape=(
            jax.ShapeDtypeStruct((owned, rows_here, lanes), bf16),
            jax.ShapeDtypeStruct((owned, width, lanes), f32),
        ),
        in_specs=[hbm] * 5,
        out_specs=(hbm, vmem),
        scratch_shapes=[
            pltpu.VMEM(solutions.shape, bf16),
            pltpu.VMEM(mass_blocks.shape, bf16),
            pltpu.VMEM((2 * MOMENTS * TILE, points * TILE), bf16),
            pltpu.VMEM((owned, rows_here, lanes), bf16),
            pltpu.VMEM((owned, rows_here, lanes), bf16),
            pltpu.VMEM((owned, rows_here, lanes), bf16),
            pltpu.VMEM((owned, rows_here, lanes), bf16),
            pltpu.VMEM(quarter, f32),
            pltpu.VMEM(quarter, RS_TYPE),
            pltpu.VMEM(quarter, RS_TYPE),
            pltpu.VMEM(quarter[1:], f32),
            pltpu.VMEM(quarter[1:], f32),
            pltpu.VMEM(quarter, AG_TYPE),
            pltpu.VMEM((LATE, block_size, lanes), bf16),
            pltpu.SMEM(point_of_slot.shape, jnp.int32),
            pltpu.SMEM(block_cols.shape, jnp.int32),
            pltpu.VMEM(block_cols.shape, jnp.int32),
            pltpu.VMEM((width // 2, rows_here), bf16),
            pltpu.VMEM((span, slots * TILE), f32),
            pltpu.VMEM((3 * span, width // 2, block_size), f32),
            pltpu.VMEM((span, width // 2, block_size), bf16),
            pltpu.VMEM((span, width // 2, block_size), bf16),
            pltpu.VMEM((span, width // 2, block_size), bf16),
            pltpu.VMEM((span, width // 2, block_size), bf16),
            pltpu.VMEM((2, span, width // 2, block_size), f32),
        ]
        + [pltpu.VMEM((3 * span, block_size, lanes), bf16) for _ in range(owned)]
        + [
            dma((chunks,)), dma((2,)), dma((4,)), dma((owned,)), dma((chunks,)), dma((chunks,)),
            dma((pieces,)), dma((pieces,)), dma((pieces,)), dma((pieces,)), dma((3,)), dma((3,)),
            dma((parts,)), dma((parts,)), dma((2,)), dma((parts,)), dma((parts,)), pltpu.SemaphoreType.REGULAR((ROUNDS,)),
        ],
        compiler_params=pltpu.CompilerParams(
            collective_id=0, has_side_effects=True, vmem_limit_bytes=48 * 1024 * 1024
        ),
    )(*[
        pltpu.with_memory_space_constraint(x, pltpu.HBM)
        for x in (point_of_slot, block_cols, sources.T, solutions, mass_blocks)
    ])
    if not reduce_here:
        reduced = lax.psum(reduced, "rows")
    return mass_applied, reduced


def solution(mesh):
    in_specs = (
        P("quad", ("group", "rows"), None),
        P(("group", "quad")),
        P(("group", "rows"), None, None, None),
        P(("group", "rows"), None),
        P(("group", "rows"), None),
    )
    out_specs = (P("quad", ("group", "rows"), None), P(("group", "quad"), None, None))
    step = functools.partial(local, mesh.shape["rows"], mesh.shape["quad"])
    return jax.shard_map(step, mesh=mesh, in_specs=in_specs, out_specs=out_specs, check_vma=False)
```

```python
import contextlib
import functools
import math

import jax
import jax.numpy as jnp
from jax import lax
from jax.experimental import pallas as pl
from jax.experimental.pallas import tpu as pltpu
from jax.sharding import PartitionSpec as P

MOMENTS = 8
TILE = 16
FIRST_WINDOW = 6
WINDOW = 6
LAST_WINDOW = 4
V_PARTS = 5
LATE = 3
ROUNDS = 2
NAMED = False
RS_TYPE = jnp.bfloat16
AG_TYPE = jnp.bfloat16
MESH = pl.DeviceIdType.MESH


def chunk_cuts(span, chunk_blocks):
    return [0, 1] + list(range(chunk_blocks, span + 1, chunk_blocks))


def part_of(name):
    return jax.named_scope(name) if NAMED else contextlib.nullcontext()


def kernel(
    n, quads, span, owned, points, chunk_blocks, reduce_here,
    point_hbm, cols_hbm, sources_hbm, sol_hbm, mass_hbm,
    out, red_out,
    sol, mass, weight, own, theirs, received, term, rs_send_buf, rs_buf, pair_send, pair_recv, red, late,
    point_ref, cols_ref, cols_vec, sources, places, v, back_send, back_recv, cross_send, cross_recv, halves, *rest,
):
    panels = rest[:owned]
    (sol_sem, mass_sem, small_sem, q_send, q_recv, x_send, x_recv, f_send, f_recv,
     b_send, b_recv, c_send, c_recv, h_sem, rs_send, rs_recv, pair_out, pair_in, ag_send, ag_recv, hello) = rest[owned:]
    me = lax.axis_index("rows")
    quad = lax.axis_index("quad")
    rows_here, lanes = sol.shape[1:]
    half = lanes // 2
    width = 2 * sources.shape[0]
    block = rows_here // span
    slots = mass.shape[1]
    cuts = chunk_cuts(span, chunk_blocks)
    chunks = len(cuts) - 1
    bf16, f32 = jnp.bfloat16, jnp.float32
    odd = lax.rem(me, 2)
    partner = me + 1 - 2 * odd
    onward = lax.rem(me + 2 - 4 * odd + n, n)
    behind = lax.rem(me - 2 + 4 * odd + n, n)
    sends_on = jnp.where(odd == 1, me - 2 >= 0, me + 2 < n)
    gets_on = jnp.where(odd == 1, me + 2 < n, me - 2 >= 0)
    there = 2 * span * odd
    here = 2 * span - there

    def rows_of(c):
        return pl.ds(cuts[c] * block, (cuts[c + 1] - cuts[c]) * block)

    def sol_copy(c):
        rows = rows_of(c)
        return pltpu.make_async_copy(sol_hbm.at[:, rows], sol.at[:, rows], sol_sem.at[c])

    halfway = span // 2
    mass_copies = [
        pltpu.make_async_copy(mass_hbm.at[rows], mass.at[rows], mass_sem.at[h])
        for h, rows in ((0, pl.ds(0, halfway)), (1, pl.ds(halfway, span - halfway)))
    ]
    point_copy = pltpu.make_async_copy(point_hbm, point_ref, small_sem.at[0])
    cols_copy = pltpu.make_async_copy(cols_hbm, cols_ref, small_sem.at[1])
    vec_copy = pltpu.make_async_copy(cols_hbm, cols_vec, small_sem.at[2])
    share = pl.ds(pl.multiple_of(quad * (width // 2), width // 2), width // 2)
    sources_copy = pltpu.make_async_copy(sources_hbm.at[share], sources, small_sem.at[3])
    point_copy.start()
    queue = [sol_copy(c) for c in range(chunks)] + [cols_copy, vec_copy, sources_copy, *mass_copies]
    later = [queue[3 + c:4 + c] for c in range(chunks)]
    later[chunks - 3], later[chunks - 2], later[chunks - 1] = queue[chunks:-1], queue[-1:], []
    for copy in queue[:3]:
        copy.start()

    barrier = pltpu.get_barrier_semaphore()

    def greet(semaphore):
        pl.semaphore_signal(semaphore, inc=1, device_id={"rows": partner}, device_id_type=MESH)

        @pl.when(sends_on)
        def _():
            pl.semaphore_signal(semaphore, inc=1, device_id={"rows": onward}, device_id_type=MESH)

        @pl.when(gets_on)
        def _():
            pl.semaphore_signal(semaphore, inc=1, device_id={"rows": behind}, device_id_type=MESH)

    greeted = 1 + sends_on.astype(jnp.int32) + gets_on.astype(jnp.int32)
    pl.semaphore_signal(barrier, inc=1, device_id={"quad": 1 - quad}, device_id_type=MESH)
    greet(barrier)

    part = lax.broadcasted_iota(jnp.int32, (2 * 2 * owned * TILE, 2 * 2 * owned), 0)
    spread = jnp.where(
        part // TILE == lax.broadcasted_iota(jnp.int32, part.shape, 1), 1.0, 0.0
    ).astype(bf16)
    across = lax.broadcasted_iota(jnp.int32, (points * TILE, points), 0)
    spread_points = jnp.where(
        across // TILE == lax.broadcasted_iota(jnp.int32, across.shape, 1), 1.0, 0.0
    ).astype(bf16)
    same = lax.rem(lax.broadcasted_iota(jnp.int32, (part.shape[0], across.shape[0]), 0), TILE) == lax.rem(
        lax.broadcasted_iota(jnp.int32, (part.shape[0], across.shape[0]), 1), TILE
    )
    total_points = points * quads
    shape = (2 * MOMENTS, points)
    row = lax.broadcasted_iota(jnp.int32, shape, 0)
    lane = lax.broadcasted_iota(jnp.int32, shape, 1)
    moment = lax.rem(row + owned * quad, MOMENTS) + 1
    point_copy.wait()
    point = jnp.zeros(shape, jnp.int32)
    for s in range(points):
        point = jnp.where(lane == s, point_ref[s], point)
    turn = lax.rem((2 * point + 1) * moment, 2 * total_points)
    turn = jnp.where(turn >= total_points, turn - 2 * total_points, turn)
    angle = turn.astype(f32) * (math.pi / total_points)
    trig = (jnp.where(row < MOMENTS, jnp.cos(angle), jnp.sin(angle)) / total_points).astype(bf16)
    tall = jnp.dot(spread, trig, preferred_element_type=f32).astype(bf16)
    wide = lax.dot_general(tall, spread_points, (((1,), (1,)), ((), ())), preferred_element_type=f32)
    weight[...] = jnp.where(same, wide, 0.0).astype(bf16)

    def quad_copy(c):
        rows = rows_of(c)
        return pltpu.make_async_remote_copy(
            src_ref=theirs.at[:, rows], dst_ref=received.at[:, rows],
            send_sem=q_send.at[c], recv_sem=q_recv.at[c],
            device_id={"quad": 1 - quad}, device_id_type=MESH,
        )

    last = owned - 1
    order = [(0, cuts[c], cuts[c + 1] - cuts[c]) for c in range(chunks)]
    order += [(k, b, chunk_blocks) for k in range(1, last) for b in range(0, span, chunk_blocks)]
    order += [(last, b, 1) for b in range(span)]
    pieces = len(order)
    starts = [[] for _ in range(pieces)]
    first_begun = next(c for c in range(chunks) if cuts[c + 1] >= FIRST_WINDOW) + 1
    begun, sent_blocks = first_begun, [sum(count for _, _, count in order[:q + 1]) for q in range(pieces)]
    for q in range(pieces):
        while begun < pieces:
            limit = FIRST_WINDOW if q < 3 else WINDOW if order[begun][0] < last else LAST_WINDOW
            if sent_blocks[begun] - sent_blocks[q] > limit:
                break
            starts[q].append(begun)
            begun += 1

    def blocks_of(q, parity):
        k, first, count = order[q]
        if k == last:
            first = first + parity * (span - count - 2 * first)
        return first, count

    def at(q, base, parity):
        first, count = blocks_of(q, parity)
        return panels[order[q][0]].at[pl.ds(base + first, count)]

    def cross(q, base):
        return pltpu.make_async_remote_copy(
            src_ref=at(q, span, odd), dst_ref=at(q, base, odd),
            send_sem=x_send.at[q], recv_sem=x_recv.at[q],
            device_id={"rows": partner}, device_id_type=MESH,
        )

    def forward(q):
        k, first, count = order[q]
        if k == last and first >= span - LATE:
            target = late.at[pl.ds(first - (span - LATE), count)]
        else:
            target = at(q, there, 1 - odd)
        return pltpu.make_async_remote_copy(
            src_ref=at(q, here, 1 - odd), dst_ref=target,
            send_sem=f_send.at[q], recv_sem=f_recv.at[q],
            device_id={"rows": onward}, device_id_type=MESH,
        )

    def relay(q):
        with part_of(f"relay_{q}_sent"):
            cross(q, there).wait_send()
            for p in starts[q]:
                cross(p, there).start()
        with part_of(f"relay_{q}_here"):
            cross(q, here).wait_recv()

        @pl.when(sends_on)
        def _():
            forward(q).start()

    def arrived(k, first=0, stop=None):
        with part_of(f"arrived_{k}"):

            @pl.when(gets_on)
            def _():
                for q in range(pieces):
                    if order[q][0] == k and first <= order[q][1] < (span if stop is None else stop):
                        forward(q).wait_recv()

    def place_late():
        @pl.when(gets_on)
        def _():
            for q in range(pieces):
                if order[q][0] == last and order[q][1] >= span - LATE:
                    first, count = blocks_of(q, 1 - odd)
                    panels[last][pl.ds(there + first, count)] = late[
                        pl.ds(order[q][1] - (span - LATE), count)
                    ]

    def weigh(c):
        for g in range(cuts[c] * block // (2 * TILE), cuts[c + 1] * block // (2 * TILE)):
            first = g * 2 * TILE
            second = first + TILE
            stacked = jnp.concatenate(
                [
                    sol[:, pl.ds(first, TILE), :].reshape(points * TILE, lanes),
                    sol[:, pl.ds(second, TILE), :].reshape(points * TILE, lanes),
                ],
                axis=1,
            )
            z = jnp.dot(weight[...], stacked, preferred_element_type=f32)
            height = 2 * owned * TILE
            negative = lax.broadcasted_iota(jnp.int32, (height, lanes), 1) < half
            for h, start in ((0, first), (1, second)):
                straight = z[:height, h * lanes:(h + 1) * lanes]
                crossed = pltpu.roll(z[height:, h * lanes:(h + 1) * lanes], half, 1)
                value = straight + jnp.where(negative, -crossed, crossed)
                value = value.astype(bf16).reshape(2 * owned, TILE, lanes)
                own[:, pl.ds(start, TILE), :] = value[:owned]
                theirs[:, pl.ds(start, TILE), :] = value[owned:]

    def add_up(c):
        quad_copy(c).wait_recv()
        for k in range(owned):
            for b in range(cuts[c], cuts[c + 1]):
                rows = pl.ds(b * block, block)
                total = own[k, rows, :].astype(f32) + received[k, rows, :].astype(f32)
                panels[k][span + b] = total.astype(bf16)
        if c < first_begun:
            cross(c, there).start()

    for c in range(chunks):
        with part_of(f"load_{c}"):
            sol_copy(c).wait()
            for copy in later[c]:
                copy.start()
        with part_of(f"weigh_{c}"):
            weigh(c)
        if c == 0:
            with part_of("meet"):
                pl.semaphore_wait(barrier, 1 + greeted)
        quad_copy(c).start()
        if c > 0:
            with part_of(f"add_{c}"):
                add_up(c - 1)
    with part_of("add_last"):
        add_up(chunks - 1)
    offset = (me - 1) * span

    def say_hello(r):
        if reduce_here:
            greet(hello.at[r])

    def hear_hello(r):
        if reduce_here:
            pl.semaphore_wait(hello.at[r], greeted)

    v_parts = [pl.ds(p * span // V_PARTS, span // V_PARTS) for p in range(V_PARTS)]

    reach = 2 * span + 1
    tall_rows, wide_cols = reach * TILE, slots * TILE

    def prepare_places():
        vec_copy.wait()
        local_cols = (cols_vec[...] - offset).astype(f32)
        local_cols = local_cols - lax.broadcasted_iota(jnp.int32, local_cols.shape, 0).astype(f32)
        copies = jnp.where(
            lax.broadcasted_iota(jnp.int32, (slots, wide_cols), 1) // TILE
            == lax.broadcasted_iota(jnp.int32, (slots, wide_cols), 0), 1.0, 0.0
        ).astype(bf16)
        places[...] = jnp.dot(local_cols.astype(bf16), copies, preferred_element_type=f32)
        v[...] = jnp.zeros_like(v)

    def project(first, last):
        ra = lax.broadcasted_iota(jnp.int32, (tall_rows, wide_cols), 0)
        ca = lax.broadcasted_iota(jnp.int32, (tall_rows, wide_cols), 1)
        diagonal = lax.rem(ra, TILE) == lax.rem(ca, TILE)
        column = (ra // TILE).astype(f32)

        def one(i):
            rows = jnp.concatenate([mass[i, j] for j in range(slots)], axis=1)
            left = sources[:, pl.ds(pl.multiple_of(i * block, block), block)]
            product = jnp.dot(left, rows, preferred_element_type=f32).astype(bf16)
            tiles = width // 2 // TILE
            stacked = jnp.concatenate(
                [
                    jnp.concatenate(
                        [product[t * TILE:(t + 1) * TILE, j * block:(j + 1) * block] for t in range(tiles)], axis=1
                    )
                    for j in range(slots)
                ],
                axis=0,
            )
            chosen = jnp.where(diagonal & (column == places[pl.ds(i, 1), :]), 1.0, 0.0).astype(bf16)
            summed = jnp.dot(chosen, stacked, preferred_element_type=f32)
            for t in range(tiles):
                v[pl.ds(i, reach), t * TILE:(t + 1) * TILE, :] += summed[:, t * block:(t + 1) * block].reshape(
                    reach, TILE, block
                )

        def body(i, carry):
            one(first + i)
            return carry

        lax.fori_loop(0, last - first, body, 0, unroll=True)

    def back_copies():
        return [
            pltpu.make_async_remote_copy(
                src_ref=back_send.at[rows], dst_ref=back_recv.at[rows],
                send_sem=b_send.at[p], recv_sem=b_recv.at[p],
                device_id={"rows": behind}, device_id_type=MESH,
            )
            for p, rows in enumerate(v_parts)
        ]

    def cross_copies():
        return [
            pltpu.make_async_remote_copy(
                src_ref=cross_send.at[rows], dst_ref=cross_recv.at[rows],
                send_sem=c_send.at[p], recv_sem=c_recv.at[p],
                device_id={"rows": partner}, device_id_type=MESH,
            )
            for p, rows in enumerate(v_parts)
        ]

    def halves_copy(which):
        return pltpu.make_async_remote_copy(
            src_ref=halves.at[which], dst_ref=halves.at[which], send_sem=h_sem.at[0], recv_sem=h_sem.at[1],
            device_id={"quad": 1 - quad}, device_id_type=MESH,
        )

    def send_back():
        @pl.when(gets_on)
        def _():
            back_send[...] = v[pl.ds(there, span)].astype(bf16)
            for copy in back_copies():
                copy.start()

    def send_across():
        @pl.when(sends_on)
        def _():
            for copy in back_copies():
                copy.wait_recv()
            cross_send[...] = (v[pl.ds(here, span)] + back_recv[...].astype(f32)).astype(bf16)

        @pl.when(jnp.logical_not(sends_on))
        def _():
            cross_send[...] = v[pl.ds(here, span)].astype(bf16)

        for copy in cross_copies():
            copy.start()

    def share_halves():
        for copy in cross_copies():
            copy.wait_recv()
        halves[quad] = v[span:2 * span] + cross_recv[...].astype(f32)
        halves_copy(quad).start()

    layer, layers = me // 2, n // 2

    def rs_copy(o):
        return pltpu.make_async_remote_copy(
            src_ref=rs_send_buf.at[lax.rem(layer + o, layers)], dst_ref=rs_buf.at[o],
            send_sem=rs_send.at[o], recv_sem=rs_recv.at[o],
            device_id={"rows": 2 * lax.rem(layer + o, layers) + odd}, device_id_type=MESH,
        )

    def pair_copy(k):
        return pltpu.make_async_remote_copy(
            src_ref=pair_send.at[k], dst_ref=pair_recv.at[k], send_sem=pair_out.at[k], recv_sem=pair_in.at[k],
            device_id={"rows": partner}, device_id_type=MESH,
        )

    def ag_copy(o, origin):
        return pltpu.make_async_remote_copy(
            src_ref=red.at[origin], dst_ref=red.at[origin],
            send_sem=ag_send.at[o], recv_sem=ag_recv.at[o],
            device_id={"rows": 2 * lax.rem(layer + o, layers) + odd}, device_id_type=MESH,
        )

    def make_terms():
        halves_copy(1 - quad).wait_recv()
        left = jnp.concatenate(
            [jnp.concatenate([halves[h, b] for b in range(span)], axis=1) for h in range(2)], axis=0
        )
        high = left.astype(bf16)
        low = (left - high.astype(f32)).astype(bf16)
        both = jnp.concatenate([high, low], axis=0)
        for k in range(owned):
            right = panels[k][span:2 * span].reshape(rows_here, lanes)
            value = jnp.dot(both, right, preferred_element_type=f32)
            value = value[:width] + value[width:]
            if reduce_here:
                value = value.reshape(layers, width // layers, lanes)
                term[:, k] = value
                rs_send_buf[:, k] = value.astype(rs_send_buf.dtype)
            else:
                red_out[k] = value
        if reduce_here:
            for o in range(1, layers):
                rs_copy(o).start()

    def reduce():
        if reduce_here:
            total = term[layer]
            for o in range(1, layers):
                rs_copy(o).wait_recv()
                total = total + rs_buf[o].astype(f32)
            pair_send[...] = total
            for k in range(owned):
                pair_copy(k).start()

    def spread_total():
        if reduce_here:
            for k in range(owned):
                pair_copy(k).wait_recv()
            red[layer] = (pair_send[...] + pair_recv[...]).astype(red.dtype)
            for o in range(1, layers):
                ag_copy(o, layer).start()

    def apply_mass(k, begin, end):
        panel = panels[k]

        def block_row(i):
            left_side = jnp.concatenate([mass[i, j] for j in range(slots)], axis=1)
            right_side = jnp.concatenate(
                [panel[jnp.clip(cols_ref[i, j] - offset, 0, 3 * span - 1)] for j in range(slots)],
                axis=0,
            )
            value = jnp.dot(left_side, right_side, preferred_element_type=f32)
            out[k, pl.ds(pl.multiple_of(i * block, block), block), :] = value.astype(bf16)

        def body(i, carry):
            block_row(jnp.where(odd == 1, begin + i, span - 1 - begin - i))
            return carry

        with part_of(f"mass_{k}"):
            lax.fori_loop(0, end - begin, body, 0, unroll=True)

    prepare_places()
    say_hello(0)
    mass_copies[0].wait()
    sources_copy.wait()
    project(0, 2)
    relay(0)
    project(2, 3)
    relay(1)
    project(3, 5)
    relay(2)
    mass_copies[1].wait()
    project(5, 7)
    relay(3)
    project(7, 9)
    relay(4)
    project(9, span)
    send_back()
    hear_hello(0)
    say_hello(1)
    relay(5)
    cols_copy.wait()
    relay(6)
    relay(7)
    with part_of("send_across"):
        send_across()
    relay(8)
    arrived(0)
    apply_mass(0, 0, halfway)
    relay(9)
    apply_mass(0, halfway, span)
    relay(10)
    with part_of("share_halves"):
        share_halves()
    hear_hello(1)
    relay(11)
    with part_of("terms"):
        make_terms()
    relay(12)
    relay(13)
    arrived(1)
    apply_mass(1, 0, halfway)
    relay(14)
    with part_of("reduce"):
        reduce()
    relay(15)
    apply_mass(1, halfway, span)
    relay(16)
    relay(17)
    relay(18)
    with part_of("reduce"):
        spread_total()
    relay(19)
    relay(20)
    arrived(2)
    apply_mass(2, 0, halfway)
    for q in range(21, pieces):
        relay(q)
    apply_mass(2, halfway, span)
    arrived(last, 0, span - LATE)
    apply_mass(last, 0, span - LATE)
    arrived(last, span - LATE)
    place_late()
    apply_mass(last, span - LATE, span)

    with part_of("all_sent"):

        @pl.when(sends_on)
        def _():
            for q in range(pieces):
                forward(q).wait_send()

        @pl.when(gets_on)
        def _():
            for copy in back_copies():
                copy.wait_send()

        for copy in cross_copies():
            copy.wait_send()
        halves_copy(quad).wait_send()
        for c in range(chunks):
            quad_copy(c).wait_send()
    with part_of("gather"):
        if reduce_here:
            for k in range(owned):
                pair_copy(k).wait_send()
            for o in range(1, layers):
                rs_copy(o).wait_send()
                ag_copy(o, layer).wait_send()
                ag_copy(o, lax.rem(layer + layers - o, layers)).wait_recv()
            for k in range(owned):
                red_out[k] = red[:, k].astype(f32).reshape(red_out.shape[1:])


def local(n, quads, solutions, point_of_slot, mass_blocks, block_cols, sources):
    points, rows_here, lanes = solutions.shape
    width = lanes // 2
    span, slots, block_size = mass_blocks.shape[:3]
    owned = MOMENTS // quads
    chunk_blocks = 2
    chunks = len(chunk_cuts(span, chunk_blocks)) - 1
    reduce_here = n <= 8 and width % (16 * n // 2) == 0
    parts = n // 2 if reduce_here else 1
    bf16, f32 = jnp.bfloat16, jnp.float32
    dma = pltpu.SemaphoreType.DMA
    pieces = chunks + (owned - 2) * (span // chunk_blocks) + span
    quarter = (parts, owned, width // parts, lanes)
    vmem = pl.BlockSpec(memory_space=pltpu.VMEM)
    hbm = pl.BlockSpec(memory_space=pl.ANY)
    mass_applied, reduced = pl.pallas_call(
        functools.partial(kernel, n, quads, span, owned, points, chunk_blocks, reduce_here),
        out_shape=(
            jax.ShapeDtypeStruct((owned, rows_here, lanes), bf16),
            jax.ShapeDtypeStruct((owned, width, lanes), f32),
        ),
        in_specs=[hbm] * 5,
        out_specs=(vmem, vmem),
        scratch_shapes=[
            pltpu.VMEM(solutions.shape, bf16),
            pltpu.VMEM(mass_blocks.shape, bf16),
            pltpu.VMEM((2 * MOMENTS * TILE, points * TILE), bf16),
            pltpu.VMEM((owned, rows_here, lanes), bf16),
            pltpu.VMEM((owned, rows_here, lanes), bf16),
            pltpu.VMEM((owned, rows_here, lanes), bf16),
            pltpu.VMEM(quarter, f32),
            pltpu.VMEM(quarter, RS_TYPE),
            pltpu.VMEM(quarter, RS_TYPE),
            pltpu.VMEM(quarter[1:], f32),
            pltpu.VMEM(quarter[1:], f32),
            pltpu.VMEM(quarter, AG_TYPE),
            pltpu.VMEM((LATE, block_size, lanes), bf16),
            pltpu.SMEM(point_of_slot.shape, jnp.int32),
            pltpu.SMEM(block_cols.shape, jnp.int32),
            pltpu.VMEM(block_cols.shape, jnp.int32),
            pltpu.VMEM((width // 2, rows_here), bf16),
            pltpu.VMEM((span, slots * TILE), f32),
            pltpu.VMEM((3 * span, width // 2, block_size), f32),
            pltpu.VMEM((span, width // 2, block_size), bf16),
            pltpu.VMEM((span, width // 2, block_size), bf16),
            pltpu.VMEM((span, width // 2, block_size), bf16),
            pltpu.VMEM((span, width // 2, block_size), bf16),
            pltpu.VMEM((2, span, width // 2, block_size), f32),
        ]
        + [pltpu.VMEM((3 * span, block_size, lanes), bf16) for _ in range(owned)]
        + [
            dma((chunks,)), dma((2,)), dma((4,)), dma((chunks,)), dma((chunks,)),
            dma((pieces,)), dma((pieces,)), dma((pieces,)), dma((pieces,)), dma((V_PARTS,)), dma((V_PARTS,)),
            dma((V_PARTS,)), dma((V_PARTS,)), dma((2,)),
            dma((parts,)), dma((parts,)), dma((owned,)), dma((owned,)), dma((parts,)), dma((parts,)), pltpu.SemaphoreType.REGULAR((ROUNDS,)),
        ],
        compiler_params=pltpu.CompilerParams(
            collective_id=0, has_side_effects=True, vmem_limit_bytes=48 * 1024 * 1024
        ),
    )(*[
        pltpu.with_memory_space_constraint(x, pltpu.HBM)
        for x in (point_of_slot, block_cols, sources.T, solutions, mass_blocks)
    ])
    if not reduce_here:
        reduced = lax.psum(reduced, "rows")
    return mass_applied, reduced


def solution(mesh):
    in_specs = (
        P("quad", ("group", "rows"), None),
        P(("group", "quad")),
        P(("group", "rows"), None, None, None),
        P(("group", "rows"), None),
        P(("group", "rows"), None),
    )
    out_specs = (P("quad", ("group", "rows"), None), P(("group", "quad"), None, None))
    step = functools.partial(local, mesh.shape["rows"], mesh.shape["quad"])
    return jax.shard_map(step, mesh=mesh, in_specs=in_specs, out_specs=out_specs, check_vma=False)
```

```python
import contextlib
import functools
import math

import jax
import jax.numpy as jnp
from jax import lax
from jax.experimental import pallas as pl
from jax.experimental.pallas import tpu as pltpu
from jax.sharding import PartitionSpec as P

MOMENTS = 8
TILE = 16
FIRST_WINDOW = 8
WINDOW = 6
LAST_WINDOW = 4
V_PARTS = 5
LATE = 3
ROUNDS = 2
NAMED = False
RS_TYPE = jnp.bfloat16
AG_TYPE = jnp.bfloat16
MESH = pl.DeviceIdType.MESH


def chunk_cuts(span, chunk_blocks):
    return [0, 1] + list(range(chunk_blocks, span + 1, chunk_blocks))


def part_of(name):
    return jax.named_scope(name) if NAMED else contextlib.nullcontext()


def kernel(
    n, quads, span, owned, points, chunk_blocks, reduce_here,
    point_hbm, cols_hbm, sources_hbm, sol_hbm, mass_hbm,
    out, red_out,
    sol, mass, weight, own, theirs, received, term, rs_send_buf, rs_buf, pair_send, pair_recv, red, late,
    point_ref, cols_ref, cols_vec, sources, places, v, back_send, back_recv, cross_send, cross_recv, halves, *rest,
):
    panels = rest[:owned]
    (sol_sem, mass_sem, small_sem, q_send, q_recv, x_send, x_recv, f_send, f_recv,
     b_send, b_recv, c_send, c_recv, h_sem, rs_send, rs_recv, pair_out, pair_in, ag_send, ag_recv, hello) = rest[owned:]
    me = lax.axis_index("rows")
    quad = lax.axis_index("quad")
    rows_here, lanes = sol.shape[1:]
    half = lanes // 2
    width = 2 * sources.shape[0]
    block = rows_here // span
    slots = mass.shape[1]
    cuts = chunk_cuts(span, chunk_blocks)
    chunks = len(cuts) - 1
    bf16, f32 = jnp.bfloat16, jnp.float32
    odd = lax.rem(me, 2)
    partner = me + 1 - 2 * odd
    onward = lax.rem(me + 2 - 4 * odd + n, n)
    behind = lax.rem(me - 2 + 4 * odd + n, n)
    sends_on = jnp.where(odd == 1, me - 2 >= 0, me + 2 < n)
    gets_on = jnp.where(odd == 1, me + 2 < n, me - 2 >= 0)
    there = 2 * span * odd
    here = 2 * span - there

    def rows_of(c):
        return pl.ds(cuts[c] * block, (cuts[c + 1] - cuts[c]) * block)

    def sol_copy(c):
        rows = rows_of(c)
        return pltpu.make_async_copy(sol_hbm.at[:, rows], sol.at[:, rows], sol_sem.at[c])

    halfway = span // 2
    mass_copies = [
        pltpu.make_async_copy(mass_hbm.at[rows], mass.at[rows], mass_sem.at[h])
        for h, rows in ((0, pl.ds(0, halfway)), (1, pl.ds(halfway, span - halfway)))
    ]
    point_copy = pltpu.make_async_copy(point_hbm, point_ref, small_sem.at[0])
    cols_copy = pltpu.make_async_copy(cols_hbm, cols_ref, small_sem.at[1])
    vec_copy = pltpu.make_async_copy(cols_hbm, cols_vec, small_sem.at[2])
    share = pl.ds(pl.multiple_of(quad * (width // 2), width // 2), width // 2)
    sources_copy = pltpu.make_async_copy(sources_hbm.at[share], sources, small_sem.at[3])
    point_copy.start()
    queue = [sol_copy(c) for c in range(chunks)] + [cols_copy, vec_copy, sources_copy, *mass_copies]
    later = [queue[3 + c:4 + c] for c in range(chunks)]
    later[chunks - 3], later[chunks - 2], later[chunks - 1] = queue[chunks:-1], queue[-1:], []
    for copy in queue[:3]:
        copy.start()

    barrier = pltpu.get_barrier_semaphore()

    def greet(semaphore):
        pl.semaphore_signal(semaphore, inc=1, device_id={"rows": partner}, device_id_type=MESH)

        @pl.when(sends_on)
        def _():
            pl.semaphore_signal(semaphore, inc=1, device_id={"rows": onward}, device_id_type=MESH)

        @pl.when(gets_on)
        def _():
            pl.semaphore_signal(semaphore, inc=1, device_id={"rows": behind}, device_id_type=MESH)

    greeted = 1 + sends_on.astype(jnp.int32) + gets_on.astype(jnp.int32)
    pl.semaphore_signal(barrier, inc=1, device_id={"quad": 1 - quad}, device_id_type=MESH)
    greet(barrier)

    part = lax.broadcasted_iota(jnp.int32, (2 * 2 * owned * TILE, 2 * 2 * owned), 0)
    spread = jnp.where(
        part // TILE == lax.broadcasted_iota(jnp.int32, part.shape, 1), 1.0, 0.0
    ).astype(bf16)
    across = lax.broadcasted_iota(jnp.int32, (points * TILE, points), 0)
    spread_points = jnp.where(
        across // TILE == lax.broadcasted_iota(jnp.int32, across.shape, 1), 1.0, 0.0
    ).astype(bf16)
    same = lax.rem(lax.broadcasted_iota(jnp.int32, (part.shape[0], across.shape[0]), 0), TILE) == lax.rem(
        lax.broadcasted_iota(jnp.int32, (part.shape[0], across.shape[0]), 1), TILE
    )
    total_points = points * quads
    shape = (2 * MOMENTS, points)
    row = lax.broadcasted_iota(jnp.int32, shape, 0)
    lane = lax.broadcasted_iota(jnp.int32, shape, 1)
    moment = lax.rem(row + owned * quad, MOMENTS) + 1
    point_copy.wait()
    point = jnp.zeros(shape, jnp.int32)
    for s in range(points):
        point = jnp.where(lane == s, point_ref[s], point)
    turn = lax.rem((2 * point + 1) * moment, 2 * total_points)
    turn = jnp.where(turn >= total_points, turn - 2 * total_points, turn)
    angle = turn.astype(f32) * (math.pi / total_points)
    trig = (jnp.where(row < MOMENTS, jnp.cos(angle), jnp.sin(angle)) / total_points).astype(bf16)
    tall = jnp.dot(spread, trig, preferred_element_type=f32).astype(bf16)
    wide = lax.dot_general(tall, spread_points, (((1,), (1,)), ((), ())), preferred_element_type=f32)
    weight[...] = jnp.where(same, wide, 0.0).astype(bf16)

    def quad_copy(c):
        rows = rows_of(c)
        return pltpu.make_async_remote_copy(
            src_ref=theirs.at[:, rows], dst_ref=received.at[:, rows],
            send_sem=q_send.at[c], recv_sem=q_recv.at[c],
            device_id={"quad": 1 - quad}, device_id_type=MESH,
        )

    last = owned - 1
    order = [(0, cuts[c], cuts[c + 1] - cuts[c]) for c in range(chunks)]
    order += [(k, b, chunk_blocks) for k in range(1, last) for b in range(0, span, chunk_blocks)]
    order += [(last, b, 1) for b in range(span)]
    pieces = len(order)
    starts = [[] for _ in range(pieces)]
    first_begun = next(c for c in range(chunks) if cuts[c + 1] >= FIRST_WINDOW) + 1
    begun, sent_blocks = first_begun, [sum(count for _, _, count in order[:q + 1]) for q in range(pieces)]
    for q in range(pieces):
        while begun < pieces:
            limit = FIRST_WINDOW if q < 3 else WINDOW if order[begun][0] < last else LAST_WINDOW
            if sent_blocks[begun] - sent_blocks[q] > limit:
                break
            starts[q].append(begun)
            begun += 1

    def blocks_of(q, parity):
        k, first, count = order[q]
        if k == last:
            first = first + parity * (span - count - 2 * first)
        return first, count

    def at(q, base, parity):
        first, count = blocks_of(q, parity)
        return panels[order[q][0]].at[pl.ds(base + first, count)]

    def cross(q, base):
        return pltpu.make_async_remote_copy(
            src_ref=at(q, span, odd), dst_ref=at(q, base, odd),
            send_sem=x_send.at[q], recv_sem=x_recv.at[q],
            device_id={"rows": partner}, device_id_type=MESH,
        )

    def forward(q):
        k, first, count = order[q]
        if k == last and first >= span - LATE:
            target = late.at[pl.ds(first - (span - LATE), count)]
        else:
            target = at(q, there, 1 - odd)
        return pltpu.make_async_remote_copy(
            src_ref=at(q, here, 1 - odd), dst_ref=target,
            send_sem=f_send.at[q], recv_sem=f_recv.at[q],
            device_id={"rows": onward}, device_id_type=MESH,
        )

    def relay(q):
        with part_of(f"relay_{q}_sent"):
            cross(q, there).wait_send()
            for p in starts[q]:
                cross(p, there).start()
        with part_of(f"relay_{q}_here"):
            cross(q, here).wait_recv()

        @pl.when(sends_on)
        def _():
            forward(q).start()

    def arrived(k, first=0, stop=None):
        with part_of(f"arrived_{k}"):

            @pl.when(gets_on)
            def _():
                for q in range(pieces):
                    if order[q][0] == k and first <= order[q][1] < (span if stop is None else stop):
                        forward(q).wait_recv()

    def place_late():
        @pl.when(gets_on)
        def _():
            for q in range(pieces):
                if order[q][0] == last and order[q][1] >= span - LATE:
                    first, count = blocks_of(q, 1 - odd)
                    panels[last][pl.ds(there + first, count)] = late[
                        pl.ds(order[q][1] - (span - LATE), count)
                    ]

    def weigh(c):
        for g in range(cuts[c] * block // (2 * TILE), cuts[c + 1] * block // (2 * TILE)):
            first = g * 2 * TILE
            second = first + TILE
            stacked = jnp.concatenate(
                [
                    sol[:, pl.ds(first, TILE), :].reshape(points * TILE, lanes),
                    sol[:, pl.ds(second, TILE), :].reshape(points * TILE, lanes),
                ],
                axis=1,
            )
            z = jnp.dot(weight[...], stacked, preferred_element_type=f32)
            height = 2 * owned * TILE
            negative = lax.broadcasted_iota(jnp.int32, (height, lanes), 1) < half
            for h, start in ((0, first), (1, second)):
                straight = z[:height, h * lanes:(h + 1) * lanes]
                crossed = pltpu.roll(z[height:, h * lanes:(h + 1) * lanes], half, 1)
                value = straight + jnp.where(negative, -crossed, crossed)
                value = value.astype(bf16).reshape(2 * owned, TILE, lanes)
                own[:, pl.ds(start, TILE), :] = value[:owned]
                theirs[:, pl.ds(start, TILE), :] = value[owned:]

    def add_up(c):
        quad_copy(c).wait_recv()
        for k in range(owned):
            for b in range(cuts[c], cuts[c + 1]):
                rows = pl.ds(b * block, block)
                total = own[k, rows, :].astype(f32) + received[k, rows, :].astype(f32)
                panels[k][span + b] = total.astype(bf16)
        if c < first_begun:
            cross(c, there).start()

    for c in range(chunks):
        with part_of(f"load_{c}"):
            sol_copy(c).wait()
            for copy in later[c]:
                copy.start()
        with part_of(f"weigh_{c}"):
            weigh(c)
        if c == 0:
            with part_of("meet"):
                pl.semaphore_wait(barrier, 1 + greeted)
        quad_copy(c).start()
        if c > 0:
            with part_of(f"add_{c}"):
                add_up(c - 1)
    with part_of("add_last"):
        add_up(chunks - 1)
    offset = (me - 1) * span

    def say_hello(r):
        if reduce_here:
            greet(hello.at[r])

    def hear_hello(r):
        if reduce_here:
            pl.semaphore_wait(hello.at[r], greeted)

    v_parts = [pl.ds(p * span // V_PARTS, span // V_PARTS) for p in range(V_PARTS)]

    reach = 2 * span + 1
    tall_rows, wide_cols = reach * TILE, slots * TILE

    def prepare_places():
        vec_copy.wait()
        local_cols = (cols_vec[...] - offset).astype(f32)
        local_cols = local_cols - lax.broadcasted_iota(jnp.int32, local_cols.shape, 0).astype(f32)
        copies = jnp.where(
            lax.broadcasted_iota(jnp.int32, (slots, wide_cols), 1) // TILE
            == lax.broadcasted_iota(jnp.int32, (slots, wide_cols), 0), 1.0, 0.0
        ).astype(bf16)
        places[...] = jnp.dot(local_cols.astype(bf16), copies, preferred_element_type=f32)
        v[...] = jnp.zeros_like(v)

    def project(first, last):
        ra = lax.broadcasted_iota(jnp.int32, (tall_rows, wide_cols), 0)
        ca = lax.broadcasted_iota(jnp.int32, (tall_rows, wide_cols), 1)
        diagonal = lax.rem(ra, TILE) == lax.rem(ca, TILE)
        column = (ra // TILE).astype(f32)

        def one(i):
            rows = jnp.concatenate([mass[i, j] for j in range(slots)], axis=1)
            left = sources[:, pl.ds(pl.multiple_of(i * block, block), block)]
            product = jnp.dot(left, rows, preferred_element_type=f32).astype(bf16)
            tiles = width // 2 // TILE
            stacked = jnp.concatenate(
                [
                    jnp.concatenate(
                        [product[t * TILE:(t + 1) * TILE, j * block:(j + 1) * block] for t in range(tiles)], axis=1
                    )
                    for j in range(slots)
                ],
                axis=0,
            )
            chosen = jnp.where(diagonal & (column == places[pl.ds(i, 1), :]), 1.0, 0.0).astype(bf16)
            summed = jnp.dot(chosen, stacked, preferred_element_type=f32)
            for t in range(tiles):
                v[pl.ds(i, reach), t * TILE:(t + 1) * TILE, :] += summed[:, t * block:(t + 1) * block].reshape(
                    reach, TILE, block
                )

        def body(i, carry):
            one(first + i)
            return carry

        lax.fori_loop(0, last - first, body, 0, unroll=True)

    def back_copies():
        return [
            pltpu.make_async_remote_copy(
                src_ref=back_send.at[rows], dst_ref=back_recv.at[rows],
                send_sem=b_send.at[p], recv_sem=b_recv.at[p],
                device_id={"rows": behind}, device_id_type=MESH,
            )
            for p, rows in enumerate(v_parts)
        ]

    def cross_copies():
        return [
            pltpu.make_async_remote_copy(
                src_ref=cross_send.at[rows], dst_ref=cross_recv.at[rows],
                send_sem=c_send.at[p], recv_sem=c_recv.at[p],
                device_id={"rows": partner}, device_id_type=MESH,
            )
            for p, rows in enumerate(v_parts)
        ]

    def halves_copy(which):
        return pltpu.make_async_remote_copy(
            src_ref=halves.at[which], dst_ref=halves.at[which], send_sem=h_sem.at[0], recv_sem=h_sem.at[1],
            device_id={"quad": 1 - quad}, device_id_type=MESH,
        )

    def send_back():
        @pl.when(gets_on)
        def _():
            back_send[...] = v[pl.ds(there, span)].astype(bf16)
            for copy in back_copies():
                copy.start()

    def send_across():
        @pl.when(sends_on)
        def _():
            for copy in back_copies():
                copy.wait_recv()
            cross_send[...] = (v[pl.ds(here, span)] + back_recv[...].astype(f32)).astype(bf16)

        @pl.when(jnp.logical_not(sends_on))
        def _():
            cross_send[...] = v[pl.ds(here, span)].astype(bf16)

        for copy in cross_copies():
            copy.start()

    def share_halves():
        for copy in cross_copies():
            copy.wait_recv()
        halves[quad] = v[span:2 * span] + cross_recv[...].astype(f32)
        halves_copy(quad).start()

    layer, layers = me // 2, n // 2

    def rs_copy(o):
        return pltpu.make_async_remote_copy(
            src_ref=rs_send_buf.at[lax.rem(layer + o, layers)], dst_ref=rs_buf.at[o],
            send_sem=rs_send.at[o], recv_sem=rs_recv.at[o],
            device_id={"rows": 2 * lax.rem(layer + o, layers) + odd}, device_id_type=MESH,
        )

    def pair_copy(k):
        return pltpu.make_async_remote_copy(
            src_ref=pair_send.at[k], dst_ref=pair_recv.at[k], send_sem=pair_out.at[k], recv_sem=pair_in.at[k],
            device_id={"rows": partner}, device_id_type=MESH,
        )

    def ag_copy(o, origin):
        return pltpu.make_async_remote_copy(
            src_ref=red.at[origin], dst_ref=red.at[origin],
            send_sem=ag_send.at[o], recv_sem=ag_recv.at[o],
            device_id={"rows": 2 * lax.rem(layer + o, layers) + odd}, device_id_type=MESH,
        )

    def make_terms():
        halves_copy(1 - quad).wait_recv()
        left = jnp.concatenate(
            [jnp.concatenate([halves[h, b] for b in range(span)], axis=1) for h in range(2)], axis=0
        )
        high = left.astype(bf16)
        low = (left - high.astype(f32)).astype(bf16)
        both = jnp.concatenate([high, low], axis=0)
        for k in range(owned):
            right = panels[k][span:2 * span].reshape(rows_here, lanes)
            value = jnp.dot(both, right, preferred_element_type=f32)
            value = value[:width] + value[width:]
            if reduce_here:
                value = value.reshape(layers, width // layers, lanes)
                term[:, k] = value
                rs_send_buf[:, k] = value.astype(rs_send_buf.dtype)
            else:
                red_out[k] = value
        if reduce_here:
            for o in range(1, layers):
                rs_copy(o).start()

    def reduce():
        if reduce_here:
            total = term[layer]
            for o in range(1, layers):
                rs_copy(o).wait_recv()
                total = total + rs_buf[o].astype(f32)
            pair_send[...] = total
            for k in range(owned):
                pair_copy(k).start()

    def spread_total():
        if reduce_here:
            for k in range(owned):
                pair_copy(k).wait_recv()
            red[layer] = (pair_send[...] + pair_recv[...]).astype(red.dtype)
            for o in range(1, layers):
                ag_copy(o, layer).start()

    def apply_mass(k, begin, end):
        panel = panels[k]

        def block_row(i):
            left_side = jnp.concatenate([mass[i, j] for j in range(slots)], axis=1)
            right_side = jnp.concatenate(
                [panel[jnp.clip(cols_ref[i, j] - offset, 0, 3 * span - 1)] for j in range(slots)],
                axis=0,
            )
            value = jnp.dot(left_side, right_side, preferred_element_type=f32)
            out[k, pl.ds(pl.multiple_of(i * block, block), block), :] = value.astype(bf16)

        def body(i, carry):
            block_row(jnp.where(odd == 1, begin + i, span - 1 - begin - i))
            return carry

        with part_of(f"mass_{k}"):
            lax.fori_loop(0, end - begin, body, 0, unroll=True)

    prepare_places()
    say_hello(0)
    mass_copies[0].wait()
    sources_copy.wait()
    project(0, 2)
    relay(0)
    project(2, 3)
    relay(1)
    project(3, 5)
    relay(2)
    mass_copies[1].wait()
    project(5, 7)
    relay(3)
    project(7, 9)
    relay(4)
    project(9, span)
    send_back()
    hear_hello(0)
    say_hello(1)
    relay(5)
    cols_copy.wait()
    relay(6)
    relay(7)
    with part_of("send_across"):
        send_across()
    relay(8)
    arrived(0)
    apply_mass(0, 0, halfway)
    relay(9)
    apply_mass(0, halfway, span)
    relay(10)
    with part_of("share_halves"):
        share_halves()
    hear_hello(1)
    relay(11)
    with part_of("terms"):
        make_terms()
    relay(12)
    relay(13)
    arrived(1)
    apply_mass(1, 0, halfway)
    relay(14)
    with part_of("reduce"):
        reduce()
    relay(15)
    apply_mass(1, halfway, span)
    relay(16)
    relay(17)
    relay(18)
    with part_of("reduce"):
        spread_total()
    relay(19)
    relay(20)
    arrived(2)
    apply_mass(2, 0, halfway)
    for q in range(21, pieces):
        relay(q)
    apply_mass(2, halfway, span)
    arrived(last, 0, span - LATE)
    apply_mass(last, 0, span - LATE)
    arrived(last, span - LATE)
    place_late()
    apply_mass(last, span - LATE, span)

    with part_of("all_sent"):

        @pl.when(sends_on)
        def _():
            for q in range(pieces):
                forward(q).wait_send()

        @pl.when(gets_on)
        def _():
            for copy in back_copies():
                copy.wait_send()

        for copy in cross_copies():
            copy.wait_send()
        halves_copy(quad).wait_send()
        for c in range(chunks):
            quad_copy(c).wait_send()
    with part_of("gather"):
        if reduce_here:
            for k in range(owned):
                pair_copy(k).wait_send()
            for o in range(1, layers):
                rs_copy(o).wait_send()
                ag_copy(o, layer).wait_send()
                ag_copy(o, lax.rem(layer + layers - o, layers)).wait_recv()
            for k in range(owned):
                red_out[k] = red[:, k].astype(f32).reshape(red_out.shape[1:])


def local(n, quads, solutions, point_of_slot, mass_blocks, block_cols, sources):
    points, rows_here, lanes = solutions.shape
    width = lanes // 2
    span, slots, block_size = mass_blocks.shape[:3]
    owned = MOMENTS // quads
    chunk_blocks = 2
    chunks = len(chunk_cuts(span, chunk_blocks)) - 1
    reduce_here = n <= 8 and width % (16 * n // 2) == 0
    parts = n // 2 if reduce_here else 1
    bf16, f32 = jnp.bfloat16, jnp.float32
    dma = pltpu.SemaphoreType.DMA
    pieces = chunks + (owned - 2) * (span // chunk_blocks) + span
    quarter = (parts, owned, width // parts, lanes)
    vmem = pl.BlockSpec(memory_space=pltpu.VMEM)
    hbm = pl.BlockSpec(memory_space=pl.ANY)
    mass_applied, reduced = pl.pallas_call(
        functools.partial(kernel, n, quads, span, owned, points, chunk_blocks, reduce_here),
        out_shape=(
            jax.ShapeDtypeStruct((owned, rows_here, lanes), bf16),
            jax.ShapeDtypeStruct((owned, width, lanes), f32),
        ),
        in_specs=[hbm] * 5,
        out_specs=(vmem, vmem),
        scratch_shapes=[
            pltpu.VMEM(solutions.shape, bf16),
            pltpu.VMEM(mass_blocks.shape, bf16),
            pltpu.VMEM((2 * MOMENTS * TILE, points * TILE), bf16),
            pltpu.VMEM((owned, rows_here, lanes), bf16),
            pltpu.VMEM((owned, rows_here, lanes), bf16),
            pltpu.VMEM((owned, rows_here, lanes), bf16),
            pltpu.VMEM(quarter, f32),
            pltpu.VMEM(quarter, RS_TYPE),
            pltpu.VMEM(quarter, RS_TYPE),
            pltpu.VMEM(quarter[1:], f32),
            pltpu.VMEM(quarter[1:], f32),
            pltpu.VMEM(quarter, AG_TYPE),
            pltpu.VMEM((LATE, block_size, lanes), bf16),
            pltpu.SMEM(point_of_slot.shape, jnp.int32),
            pltpu.SMEM(block_cols.shape, jnp.int32),
            pltpu.VMEM(block_cols.shape, jnp.int32),
            pltpu.VMEM((width // 2, rows_here), bf16),
            pltpu.VMEM((span, slots * TILE), f32),
            pltpu.VMEM((3 * span, width // 2, block_size), f32),
            pltpu.VMEM((span, width // 2, block_size), bf16),
            pltpu.VMEM((span, width // 2, block_size), bf16),
            pltpu.VMEM((span, width // 2, block_size), bf16),
            pltpu.VMEM((span, width // 2, block_size), bf16),
            pltpu.VMEM((2, span, width // 2, block_size), f32),
        ]
        + [pltpu.VMEM((3 * span, block_size, lanes), bf16) for _ in range(owned)]
        + [
            dma((chunks,)), dma((2,)), dma((4,)), dma((chunks,)), dma((chunks,)),
            dma((pieces,)), dma((pieces,)), dma((pieces,)), dma((pieces,)), dma((V_PARTS,)), dma((V_PARTS,)),
            dma((V_PARTS,)), dma((V_PARTS,)), dma((2,)),
            dma((parts,)), dma((parts,)), dma((owned,)), dma((owned,)), dma((parts,)), dma((parts,)), pltpu.SemaphoreType.REGULAR((ROUNDS,)),
        ],
        compiler_params=pltpu.CompilerParams(
            collective_id=0, has_side_effects=True, vmem_limit_bytes=48 * 1024 * 1024
        ),
    )(*[
        pltpu.with_memory_space_constraint(x, pltpu.HBM)
        for x in (point_of_slot, block_cols, sources.T, solutions, mass_blocks)
    ])
    if not reduce_here:
        reduced = lax.psum(reduced, "rows")
    return mass_applied, reduced


def solution(mesh):
    in_specs = (
        P("quad", ("group", "rows"), None),
        P(("group", "quad")),
        P(("group", "rows"), None, None, None),
        P(("group", "rows"), None),
        P(("group", "rows"), None),
    )
    out_specs = (P("quad", ("group", "rows"), None), P(("group", "quad"), None, None))
    step = functools.partial(local, mesh.shape["rows"], mesh.shape["quad"])
    return jax.shard_map(step, mesh=mesh, in_specs=in_specs, out_specs=out_specs, check_vma=False)
```

```python
import contextlib
import functools
import math

import jax
import jax.numpy as jnp
from jax import lax
from jax.experimental import pallas as pl
from jax.experimental.pallas import tpu as pltpu
from jax.sharding import PartitionSpec as P

MOMENTS = 8
TILE = 16
FIRST_WINDOW = 8
WINDOW = 6
LAST_WINDOW = 4
V_PARTS = 5
LATE = 3
ROUNDS = 2
NAMED = False
RS_TYPE = jnp.bfloat16
AG_TYPE = jnp.bfloat16
MESH = pl.DeviceIdType.MESH


def chunk_cuts(span, chunk_blocks):
    return [0, 1] + list(range(chunk_blocks, span + 1, chunk_blocks))


def part_of(name):
    return jax.named_scope(name) if NAMED else contextlib.nullcontext()


def kernel(
    n, quads, span, owned, points, chunk_blocks, reduce_here,
    point_hbm, cols_hbm, sources_hbm, sol_hbm, mass_hbm,
    out, red_out,
    sol, mass, weight, own, theirs, received, term, rs_send_buf, rs_buf, pair_send, pair_recv, red, late,
    point_ref, cols_ref, cols_vec, sources, places, v, back_send, back_recv, cross_send, cross_recv, halves, *rest,
):
    panels = rest[:owned]
    (sol_sem, mass_sem, small_sem, q_send, q_recv, x_send, x_recv, f_send, f_recv,
     b_send, b_recv, c_send, c_recv, h_sem, rs_send, rs_recv, pair_out, pair_in, ag_send, ag_recv, hello) = rest[owned:]
    me = lax.axis_index("rows")
    quad = lax.axis_index("quad")
    rows_here, lanes = sol.shape[1:]
    half = lanes // 2
    width = 2 * sources.shape[0]
    block = rows_here // span
    slots = mass.shape[1]
    cuts = chunk_cuts(span, chunk_blocks)
    chunks = len(cuts) - 1
    bf16, f32 = jnp.bfloat16, jnp.float32
    odd = lax.rem(me, 2)
    partner = me + 1 - 2 * odd
    onward = lax.rem(me + 2 - 4 * odd + n, n)
    behind = lax.rem(me - 2 + 4 * odd + n, n)
    sends_on = jnp.where(odd == 1, me - 2 >= 0, me + 2 < n)
    gets_on = jnp.where(odd == 1, me + 2 < n, me - 2 >= 0)
    there = 2 * span * odd
    here = 2 * span - there

    def rows_of(c):
        return pl.ds(cuts[c] * block, (cuts[c + 1] - cuts[c]) * block)

    def sol_copy(c):
        rows = rows_of(c)
        return pltpu.make_async_copy(sol_hbm.at[:, rows], sol.at[:, rows], sol_sem.at[c])

    halfway = span // 2
    mass_copies = [
        pltpu.make_async_copy(mass_hbm.at[rows], mass.at[rows], mass_sem.at[h])
        for h, rows in ((0, pl.ds(0, halfway)), (1, pl.ds(halfway, span - halfway)))
    ]
    point_copy = pltpu.make_async_copy(point_hbm, point_ref, small_sem.at[0])
    cols_copy = pltpu.make_async_copy(cols_hbm, cols_ref, small_sem.at[1])
    vec_copy = pltpu.make_async_copy(cols_hbm, cols_vec, small_sem.at[2])
    share = pl.ds(pl.multiple_of(quad * (width // 2), width // 2), width // 2)
    sources_copy = pltpu.make_async_copy(sources_hbm.at[share], sources, small_sem.at[3])
    point_copy.start()
    vec_copy.start()
    queue = [sol_copy(c) for c in range(chunks)] + [cols_copy, sources_copy, *mass_copies]
    later = [queue[3 + c:4 + c] for c in range(chunks)]
    later[chunks - 3], later[chunks - 2], later[chunks - 1] = queue[chunks:-1], queue[-1:], []
    for copy in queue[:3]:
        copy.start()

    barrier = pltpu.get_barrier_semaphore()

    def greet(semaphore):
        pl.semaphore_signal(semaphore, inc=1, device_id={"rows": partner}, device_id_type=MESH)

        @pl.when(sends_on)
        def _():
            pl.semaphore_signal(semaphore, inc=1, device_id={"rows": onward}, device_id_type=MESH)

        @pl.when(gets_on)
        def _():
            pl.semaphore_signal(semaphore, inc=1, device_id={"rows": behind}, device_id_type=MESH)

    greeted = 1 + sends_on.astype(jnp.int32) + gets_on.astype(jnp.int32)
    pl.semaphore_signal(barrier, inc=1, device_id={"quad": 1 - quad}, device_id_type=MESH)
    greet(barrier)

    part = lax.broadcasted_iota(jnp.int32, (2 * 2 * owned * TILE, 2 * 2 * owned), 0)
    spread = jnp.where(
        part // TILE == lax.broadcasted_iota(jnp.int32, part.shape, 1), 1.0, 0.0
    ).astype(bf16)
    across = lax.broadcasted_iota(jnp.int32, (points * TILE, points), 0)
    spread_points = jnp.where(
        across // TILE == lax.broadcasted_iota(jnp.int32, across.shape, 1), 1.0, 0.0
    ).astype(bf16)
    same = lax.rem(lax.broadcasted_iota(jnp.int32, (part.shape[0], across.shape[0]), 0), TILE) == lax.rem(
        lax.broadcasted_iota(jnp.int32, (part.shape[0], across.shape[0]), 1), TILE
    )
    total_points = points * quads
    shape = (2 * MOMENTS, points)
    row = lax.broadcasted_iota(jnp.int32, shape, 0)
    lane = lax.broadcasted_iota(jnp.int32, shape, 1)
    moment = lax.rem(row + owned * quad, MOMENTS) + 1
    point_copy.wait()
    point = jnp.zeros(shape, jnp.int32)
    for s in range(points):
        point = jnp.where(lane == s, point_ref[s], point)
    turn = lax.rem((2 * point + 1) * moment, 2 * total_points)
    turn = jnp.where(turn >= total_points, turn - 2 * total_points, turn)
    angle = turn.astype(f32) * (math.pi / total_points)
    trig = (jnp.where(row < MOMENTS, jnp.cos(angle), jnp.sin(angle)) / total_points).astype(bf16)
    tall = jnp.dot(spread, trig, preferred_element_type=f32).astype(bf16)
    wide = lax.dot_general(tall, spread_points, (((1,), (1,)), ((), ())), preferred_element_type=f32)
    weight[...] = jnp.where(same, wide, 0.0).astype(bf16)

    def quad_copy(c):
        rows = rows_of(c)
        return pltpu.make_async_remote_copy(
            src_ref=theirs.at[:, rows], dst_ref=received.at[:, rows],
            send_sem=q_send.at[c], recv_sem=q_recv.at[c],
            device_id={"quad": 1 - quad}, device_id_type=MESH,
        )

    last = owned - 1
    order = [(0, cuts[c], cuts[c + 1] - cuts[c]) for c in range(chunks)]
    order += [(k, b, chunk_blocks) for k in range(1, last) for b in range(0, span, chunk_blocks)]
    order += [(last, b, 1) for b in range(span)]
    pieces = len(order)
    starts = [[] for _ in range(pieces)]
    first_begun = next(c for c in range(chunks) if cuts[c + 1] >= FIRST_WINDOW) + 1
    begun, sent_blocks = first_begun, [sum(count for _, _, count in order[:q + 1]) for q in range(pieces)]
    for q in range(pieces):
        while begun < pieces:
            limit = FIRST_WINDOW if q < 3 else WINDOW if order[begun][0] < last else LAST_WINDOW
            if sent_blocks[begun] - sent_blocks[q] > limit:
                break
            starts[q].append(begun)
            begun += 1

    def blocks_of(q, parity):
        k, first, count = order[q]
        if k == last:
            first = first + parity * (span - count - 2 * first)
        return first, count

    def at(q, base, parity):
        first, count = blocks_of(q, parity)
        return panels[order[q][0]].at[pl.ds(base + first, count)]

    def cross(q, base):
        return pltpu.make_async_remote_copy(
            src_ref=at(q, span, odd), dst_ref=at(q, base, odd),
            send_sem=x_send.at[q], recv_sem=x_recv.at[q],
            device_id={"rows": partner}, device_id_type=MESH,
        )

    def forward(q):
        k, first, count = order[q]
        if k == last and first >= span - LATE:
            target = late.at[pl.ds(first - (span - LATE), count)]
        else:
            target = at(q, there, 1 - odd)
        return pltpu.make_async_remote_copy(
            src_ref=at(q, here, 1 - odd), dst_ref=target,
            send_sem=f_send.at[q], recv_sem=f_recv.at[q],
            device_id={"rows": onward}, device_id_type=MESH,
        )

    def relay(q):
        with part_of(f"relay_{q}_sent"):
            cross(q, there).wait_send()
            for p in starts[q]:
                cross(p, there).start()
        with part_of(f"relay_{q}_here"):
            cross(q, here).wait_recv()

        @pl.when(sends_on)
        def _():
            forward(q).start()

    def arrived(k, first=0, stop=None):
        with part_of(f"arrived_{k}"):

            @pl.when(gets_on)
            def _():
                for q in range(pieces):
                    if order[q][0] == k and first <= order[q][1] < (span if stop is None else stop):
                        forward(q).wait_recv()

    def place_late():
        @pl.when(gets_on)
        def _():
            for q in range(pieces):
                if order[q][0] == last and order[q][1] >= span - LATE:
                    first, count = blocks_of(q, 1 - odd)
                    panels[last][pl.ds(there + first, count)] = late[
                        pl.ds(order[q][1] - (span - LATE), count)
                    ]

    def weigh(c):
        for g in range(cuts[c] * block // (2 * TILE), cuts[c + 1] * block // (2 * TILE)):
            first = g * 2 * TILE
            second = first + TILE
            stacked = jnp.concatenate(
                [
                    sol[:, pl.ds(first, TILE), :].reshape(points * TILE, lanes),
                    sol[:, pl.ds(second, TILE), :].reshape(points * TILE, lanes),
                ],
                axis=1,
            )
            z = jnp.dot(weight[...], stacked, preferred_element_type=f32)
            height = 2 * owned * TILE
            negative = lax.broadcasted_iota(jnp.int32, (height, lanes), 1) < half
            for h, start in ((0, first), (1, second)):
                straight = z[:height, h * lanes:(h + 1) * lanes]
                crossed = pltpu.roll(z[height:, h * lanes:(h + 1) * lanes], half, 1)
                value = straight + jnp.where(negative, -crossed, crossed)
                value = value.astype(bf16).reshape(2 * owned, TILE, lanes)
                own[:, pl.ds(start, TILE), :] = value[:owned]
                theirs[:, pl.ds(start, TILE), :] = value[owned:]

    def add_up(c):
        quad_copy(c).wait_recv()
        for k in range(owned):
            for b in range(cuts[c], cuts[c + 1]):
                rows = pl.ds(b * block, block)
                total = own[k, rows, :].astype(f32) + received[k, rows, :].astype(f32)
                panels[k][span + b] = total.astype(bf16)
        if c < first_begun:
            cross(c, there).start()

    offset = (me - 1) * span
    reach = 2 * span + 1
    tall_rows, wide_cols = reach * TILE, slots * TILE

    def prepare_places():
        vec_copy.wait()
        local_cols = (cols_vec[...] - offset).astype(f32)
        local_cols = local_cols - lax.broadcasted_iota(jnp.int32, local_cols.shape, 0).astype(f32)
        copies = jnp.where(
            lax.broadcasted_iota(jnp.int32, (slots, wide_cols), 1) // TILE
            == lax.broadcasted_iota(jnp.int32, (slots, wide_cols), 0), 1.0, 0.0
        ).astype(bf16)
        places[...] = jnp.dot(local_cols.astype(bf16), copies, preferred_element_type=f32)
        v[...] = jnp.zeros_like(v)

    prepare_places()
    for c in range(chunks):
        with part_of(f"load_{c}"):
            sol_copy(c).wait()
            for copy in later[c]:
                copy.start()
        with part_of(f"weigh_{c}"):
            weigh(c)
        if c == 0:
            with part_of("meet"):
                pl.semaphore_wait(barrier, 1 + greeted)
        quad_copy(c).start()
        if c > 0:
            with part_of(f"add_{c}"):
                add_up(c - 1)
    with part_of("add_last"):
        add_up(chunks - 1)

    def say_hello(r):
        if reduce_here:
            greet(hello.at[r])

    def hear_hello(r):
        if reduce_here:
            pl.semaphore_wait(hello.at[r], greeted)

    v_parts = [pl.ds(p * span // V_PARTS, span // V_PARTS) for p in range(V_PARTS)]


    def project(first, last):
        ra = lax.broadcasted_iota(jnp.int32, (tall_rows, wide_cols), 0)
        ca = lax.broadcasted_iota(jnp.int32, (tall_rows, wide_cols), 1)
        diagonal = lax.rem(ra, TILE) == lax.rem(ca, TILE)
        column = (ra // TILE).astype(f32)

        def one(i):
            rows = jnp.concatenate([mass[i, j] for j in range(slots)], axis=1)
            left = sources[:, pl.ds(pl.multiple_of(i * block, block), block)]
            product = jnp.dot(left, rows, preferred_element_type=f32).astype(bf16)
            tiles = width // 2 // TILE
            stacked = jnp.concatenate(
                [
                    jnp.concatenate(
                        [product[t * TILE:(t + 1) * TILE, j * block:(j + 1) * block] for t in range(tiles)], axis=1
                    )
                    for j in range(slots)
                ],
                axis=0,
            )
            chosen = jnp.where(diagonal & (column == places[pl.ds(i, 1), :]), 1.0, 0.0).astype(bf16)
            summed = jnp.dot(chosen, stacked, preferred_element_type=f32)
            for t in range(tiles):
                v[pl.ds(i, reach), t * TILE:(t + 1) * TILE, :] += summed[:, t * block:(t + 1) * block].reshape(
                    reach, TILE, block
                )

        def body(i, carry):
            one(first + i)
            return carry

        lax.fori_loop(0, last - first, body, 0, unroll=True)

    def back_copies():
        return [
            pltpu.make_async_remote_copy(
                src_ref=back_send.at[rows], dst_ref=back_recv.at[rows],
                send_sem=b_send.at[p], recv_sem=b_recv.at[p],
                device_id={"rows": behind}, device_id_type=MESH,
            )
            for p, rows in enumerate(v_parts)
        ]

    def cross_copies():
        return [
            pltpu.make_async_remote_copy(
                src_ref=cross_send.at[rows], dst_ref=cross_recv.at[rows],
                send_sem=c_send.at[p], recv_sem=c_recv.at[p],
                device_id={"rows": partner}, device_id_type=MESH,
            )
            for p, rows in enumerate(v_parts)
        ]

    def halves_copy(which):
        return pltpu.make_async_remote_copy(
            src_ref=halves.at[which], dst_ref=halves.at[which], send_sem=h_sem.at[0], recv_sem=h_sem.at[1],
            device_id={"quad": 1 - quad}, device_id_type=MESH,
        )

    def send_back():
        @pl.when(gets_on)
        def _():
            back_send[...] = v[pl.ds(there, span)].astype(bf16)
            for copy in back_copies():
                copy.start()

    def send_across():
        @pl.when(sends_on)
        def _():
            for copy in back_copies():
                copy.wait_recv()
            cross_send[...] = (v[pl.ds(here, span)] + back_recv[...].astype(f32)).astype(bf16)

        @pl.when(jnp.logical_not(sends_on))
        def _():
            cross_send[...] = v[pl.ds(here, span)].astype(bf16)

        for copy in cross_copies():
            copy.start()

    def share_halves():
        for copy in cross_copies():
            copy.wait_recv()
        halves[quad] = v[span:2 * span] + cross_recv[...].astype(f32)
        halves_copy(quad).start()

    layer, layers = me // 2, n // 2

    def rs_copy(o):
        return pltpu.make_async_remote_copy(
            src_ref=rs_send_buf.at[lax.rem(layer + o, layers)], dst_ref=rs_buf.at[o],
            send_sem=rs_send.at[o], recv_sem=rs_recv.at[o],
            device_id={"rows": 2 * lax.rem(layer + o, layers) + odd}, device_id_type=MESH,
        )

    def pair_copy(k):
        return pltpu.make_async_remote_copy(
            src_ref=pair_send.at[k], dst_ref=pair_recv.at[k], send_sem=pair_out.at[k], recv_sem=pair_in.at[k],
            device_id={"rows": partner}, device_id_type=MESH,
        )

    def ag_copy(o, origin):
        return pltpu.make_async_remote_copy(
            src_ref=red.at[origin], dst_ref=red.at[origin],
            send_sem=ag_send.at[o], recv_sem=ag_recv.at[o],
            device_id={"rows": 2 * lax.rem(layer + o, layers) + odd}, device_id_type=MESH,
        )

    def make_terms():
        halves_copy(1 - quad).wait_recv()
        left = jnp.concatenate(
            [jnp.concatenate([halves[h, b] for b in range(span)], axis=1) for h in range(2)], axis=0
        )
        high = left.astype(bf16)
        low = (left - high.astype(f32)).astype(bf16)
        both = jnp.concatenate([high, low], axis=0)
        for k in range(owned):
            right = panels[k][span:2 * span].reshape(rows_here, lanes)
            value = jnp.dot(both, right, preferred_element_type=f32)
            value = value[:width] + value[width:]
            if reduce_here:
                value = value.reshape(layers, width // layers, lanes)
                term[:, k] = value
                rs_send_buf[:, k] = value.astype(rs_send_buf.dtype)
            else:
                red_out[k] = value
        if reduce_here:
            for o in range(1, layers):
                rs_copy(o).start()

    def reduce():
        if reduce_here:
            total = term[layer]
            for o in range(1, layers):
                rs_copy(o).wait_recv()
                total = total + rs_buf[o].astype(f32)
            pair_send[...] = total
            for k in range(owned):
                pair_copy(k).start()

    def spread_total():
        if reduce_here:
            for k in range(owned):
                pair_copy(k).wait_recv()
            red[layer] = (pair_send[...] + pair_recv[...]).astype(red.dtype)
            for o in range(1, layers):
                ag_copy(o, layer).start()

    def apply_mass(k, begin, end):
        panel = panels[k]

        def block_row(i):
            left_side = jnp.concatenate([mass[i, j] for j in range(slots)], axis=1)
            right_side = jnp.concatenate(
                [panel[jnp.clip(cols_ref[i, j] - offset, 0, 3 * span - 1)] for j in range(slots)],
                axis=0,
            )
            value = jnp.dot(left_side, right_side, preferred_element_type=f32)
            out[k, pl.ds(pl.multiple_of(i * block, block), block), :] = value.astype(bf16)

        def body(i, carry):
            block_row(jnp.where(odd == 1, begin + i, span - 1 - begin - i))
            return carry

        with part_of(f"mass_{k}"):
            lax.fori_loop(0, end - begin, body, 0, unroll=True)

    say_hello(0)
    mass_copies[0].wait()
    sources_copy.wait()
    project(0, 2)
    relay(0)
    project(2, 3)
    relay(1)
    project(3, 5)
    relay(2)
    mass_copies[1].wait()
    project(5, 7)
    relay(3)
    project(7, 9)
    relay(4)
    project(9, span)
    send_back()
    hear_hello(0)
    say_hello(1)
    relay(5)
    cols_copy.wait()
    relay(6)
    relay(7)
    with part_of("send_across"):
        send_across()
    relay(8)
    arrived(0)
    apply_mass(0, 0, halfway)
    relay(9)
    apply_mass(0, halfway, span)
    relay(10)
    with part_of("share_halves"):
        share_halves()
    hear_hello(1)
    relay(11)
    with part_of("terms"):
        make_terms()
    relay(12)
    relay(13)
    arrived(1)
    apply_mass(1, 0, halfway)
    relay(14)
    with part_of("reduce"):
        reduce()
    relay(15)
    apply_mass(1, halfway, span)
    relay(16)
    relay(17)
    relay(18)
    with part_of("reduce"):
        spread_total()
    relay(19)
    relay(20)
    arrived(2)
    apply_mass(2, 0, halfway)
    for q in range(21, pieces):
        relay(q)
    apply_mass(2, halfway, span)
    arrived(last, 0, span - LATE)
    apply_mass(last, 0, span - LATE)
    arrived(last, span - LATE)
    place_late()
    apply_mass(last, span - LATE, span)

    with part_of("all_sent"):

        @pl.when(sends_on)
        def _():
            for q in range(pieces):
                forward(q).wait_send()

        @pl.when(gets_on)
        def _():
            for copy in back_copies():
                copy.wait_send()

        for copy in cross_copies():
            copy.wait_send()
        halves_copy(quad).wait_send()
        for c in range(chunks):
            quad_copy(c).wait_send()
    with part_of("gather"):
        if reduce_here:
            for k in range(owned):
                pair_copy(k).wait_send()
            for o in range(1, layers):
                rs_copy(o).wait_send()
                ag_copy(o, layer).wait_send()
                ag_copy(o, lax.rem(layer + layers - o, layers)).wait_recv()
            for k in range(owned):
                red_out[k] = red[:, k].astype(f32).reshape(red_out.shape[1:])


def local(n, quads, solutions, point_of_slot, mass_blocks, block_cols, sources):
    points, rows_here, lanes = solutions.shape
    width = lanes // 2
    span, slots, block_size = mass_blocks.shape[:3]
    owned = MOMENTS // quads
    chunk_blocks = 2
    chunks = len(chunk_cuts(span, chunk_blocks)) - 1
    reduce_here = n <= 8 and width % (16 * n // 2) == 0
    parts = n // 2 if reduce_here else 1
    bf16, f32 = jnp.bfloat16, jnp.float32
    dma = pltpu.SemaphoreType.DMA
    pieces = chunks + (owned - 2) * (span // chunk_blocks) + span
    quarter = (parts, owned, width // parts, lanes)
    vmem = pl.BlockSpec(memory_space=pltpu.VMEM)
    hbm = pl.BlockSpec(memory_space=pl.ANY)
    mass_applied, reduced = pl.pallas_call(
        functools.partial(kernel, n, quads, span, owned, points, chunk_blocks, reduce_here),
        out_shape=(
            jax.ShapeDtypeStruct((owned, rows_here, lanes), bf16),
            jax.ShapeDtypeStruct((owned, width, lanes), f32),
        ),
        in_specs=[hbm] * 5,
        out_specs=(vmem, vmem),
        scratch_shapes=[
            pltpu.VMEM(solutions.shape, bf16),
            pltpu.VMEM(mass_blocks.shape, bf16),
            pltpu.VMEM((2 * MOMENTS * TILE, points * TILE), bf16),
            pltpu.VMEM((owned, rows_here, lanes), bf16),
            pltpu.VMEM((owned, rows_here, lanes), bf16),
            pltpu.VMEM((owned, rows_here, lanes), bf16),
            pltpu.VMEM(quarter, f32),
            pltpu.VMEM(quarter, RS_TYPE),
            pltpu.VMEM(quarter, RS_TYPE),
            pltpu.VMEM(quarter[1:], f32),
            pltpu.VMEM(quarter[1:], f32),
            pltpu.VMEM(quarter, AG_TYPE),
            pltpu.VMEM((LATE, block_size, lanes), bf16),
            pltpu.SMEM(point_of_slot.shape, jnp.int32),
            pltpu.SMEM(block_cols.shape, jnp.int32),
            pltpu.VMEM(block_cols.shape, jnp.int32),
            pltpu.VMEM((width // 2, rows_here), bf16),
            pltpu.VMEM((span, slots * TILE), f32),
            pltpu.VMEM((3 * span, width // 2, block_size), f32),
            pltpu.VMEM((span, width // 2, block_size), bf16),
            pltpu.VMEM((span, width // 2, block_size), bf16),
            pltpu.VMEM((span, width // 2, block_size), bf16),
            pltpu.VMEM((span, width // 2, block_size), bf16),
            pltpu.VMEM((2, span, width // 2, block_size), f32),
        ]
        + [pltpu.VMEM((3 * span, block_size, lanes), bf16) for _ in range(owned)]
        + [
            dma((chunks,)), dma((2,)), dma((4,)), dma((chunks,)), dma((chunks,)),
            dma((pieces,)), dma((pieces,)), dma((pieces,)), dma((pieces,)), dma((V_PARTS,)), dma((V_PARTS,)),
            dma((V_PARTS,)), dma((V_PARTS,)), dma((2,)),
            dma((parts,)), dma((parts,)), dma((owned,)), dma((owned,)), dma((parts,)), dma((parts,)), pltpu.SemaphoreType.REGULAR((ROUNDS,)),
        ],
        compiler_params=pltpu.CompilerParams(
            collective_id=0, has_side_effects=True, vmem_limit_bytes=48 * 1024 * 1024
        ),
    )(*[
        pltpu.with_memory_space_constraint(x, pltpu.HBM)
        for x in (point_of_slot, block_cols, sources.T, solutions, mass_blocks)
    ])
    if not reduce_here:
        reduced = lax.psum(reduced, "rows")
    return mass_applied, reduced


def solution(mesh):
    in_specs = (
        P("quad", ("group", "rows"), None),
        P(("group", "quad")),
        P(("group", "rows"), None, None, None),
        P(("group", "rows"), None),
        P(("group", "rows"), None),
    )
    out_specs = (P("quad", ("group", "rows"), None), P(("group", "quad"), None, None))
    step = functools.partial(local, mesh.shape["rows"], mesh.shape["quad"])
    return jax.shard_map(step, mesh=mesh, in_specs=in_specs, out_specs=out_specs, check_vma=False)
```
